256 devices in a mesh: chain: 64 (over y, z, core), sub: 4 (over x).
Axes of the slice: x: 4, y: 4, z: 8, core: 2. Of those that a mesh axis runs over, the one named last changes fastest.
Arguments:
- rhs: float32 [1536, 5, 8, 512], P('chain', None, None, 'sub'), may hold values from -100 to 100
- diag_block: float32 [1536, 5, 5, 512], P('chain', None, None, 'sub')
- diag_inverse: float32 [1536, 5, 5, 512], P('chain', None, None, 'sub'), as said below
- lower_coef: float32 [1536, 2, 5, 5, 512], P('chain', None, None, None, 'sub')
- upper_coef: float32 [1536, 2, 5, 5, 512], P('chain', None, None, None, 'sub')
- side_coef: float32 [1536, 2, 5, 5, 512], P('chain', None, None, None, 'sub')
- lower_cols: int32 [1536, 2], P('chain'), may hold values from -3 to 1534, as said below
- upper_cols: int32 [1536, 2], P('chain'), may hold values from 1 to 1538, as said below
- counts: int32 [1536, 2], P('chain'), may hold values from 1 to 2
Outputs:
- correction: float32 [1536, 5, 8, 512], P('chain', None, None, 'sub')
- residual_unit: float32 [1536, 5, 8, 512], P('chain', None, None, 'sub')
The draws below stay inside these ranges and needn't reach their ends.
Inputs may be any that keep to these rules, and one draw needn't show every extreme that they name: lower_cols[b, k] = b - d with d from 1 to 3, the two slots of a block differ, and some block has d = 3. upper_cols[b, k] = b + d with d from 1 to 3, the two slots of a block differ, and some block has d = 3. diag_inverse is the inverse of diag_block at every block and cell.
All inputs are finite; a program needn't handle non-finite values.
Results may differ from the reference program's by a relative error of at most 0.0003.
Values sent between devices are 32-bit elements; how exact they have to be, the bound alone decides.
A program may use at most 128 MiB of HBM per device.

```python
import math
import jax
import jax.numpy as jnp
from jax import lax

VARS = 5
RHS = 8
REACH = 3
SLOTS = 2
BLOCK_TOTAL = 1536
NCELL = 512


def layout_ints(key):
    random_keys = jax.random.split(jax.random.fold_in(key, 11), 4)
    rows = jnp.arange(BLOCK_TOTAL, dtype=jnp.int32)

    def offsets(subkey):
        key_a, key_b, key_c, key_d = jax.random.split(subkey, 4)
        omit = jax.random.randint(key_a, (BLOCK_TOTAL,), 0, 3)
        first = (omit + 1) % 3 + 1
        second = (omit + 2) % 3 + 1
        flip = jax.random.randint(key_b, (BLOCK_TOTAL,), 0, 2)
        slot_one = jnp.where(flip == 1, second, first)
        slot_two = jnp.where(flip == 1, first, second)
        forced = (jax.random.randint(key_c, (BLOCK_TOTAL,), 0, 7) == 0) | (rows == BLOCK_TOTAL // 2)
        other = jax.random.randint(key_d, (BLOCK_TOTAL,), 1, REACH)
        slot_one = jnp.where(forced, REACH, slot_one)
        slot_two = jnp.where(forced, other, slot_two)
        return jnp.stack([slot_one, slot_two], 1).astype(jnp.int32)
    low_off = offsets(random_keys[0])
    up_off = offsets(random_keys[1])
    level = 1 + rows // 16 % 3
    count_low = 1 + (jax.random.randint(random_keys[2], (BLOCK_TOTAL,), 0, 4) < level).astype(jnp.int32)
    count_up = 1 + (jax.random.randint(random_keys[3], (BLOCK_TOTAL,), 0, 4) < level).astype(jnp.int32)
    return (low_off, up_off, jnp.stack([count_low, count_up], 1).astype(jnp.int32))


def decay(key, tag):
    random_keys = jax.random.split(jax.random.fold_in(key, tag), 5)
    share = 0.5
    slow = jax.random.uniform(random_keys[0], (NCELL,)) < share
    long_horizon = BLOCK_TOTAL * jnp.exp(jax.random.uniform(random_keys[1], (NCELL,), minval=0.0, maxval=math.log(4.0)))
    short_t = jnp.exp(jax.random.uniform(random_keys[2], (NCELL,), minval=math.log(30.0), maxval=math.log(50.0)))
    base = jnp.where(slow, long_horizon, short_t)
    factor = jnp.exp(jax.random.uniform(random_keys[3], (BLOCK_TOTAL, NCELL), minval=math.log(0.7), maxval=math.log(1.4)))
    tau = base[None, :] * factor
    grouped_rows = jax.random.randint(random_keys[4], (3,), 0, BLOCK_TOTAL)
    block_touched = jnp.any(jnp.arange(BLOCK_TOTAL)[:, None] == grouped_rows[None, :], axis=1)
    rho = jnp.exp(-1.0 / tau) * jnp.where(block_touched, 0.65, 1.0)[:, None]
    return (rho, tau)


def diag_pair(key):
    rho, tau = decay(key, 21)
    scale = jnp.sqrt(tau)
    noise = 0.1 * jax.random.normal(jax.random.fold_in(key, 22), (BLOCK_TOTAL, NCELL, 5, 5))
    dmat = scale[:, :, None, None] * (jnp.eye(5, dtype=jnp.float32) + noise)
    return (dmat, jnp.linalg.inv(dmat))


def to_layout(matrix):
    return jnp.transpose(matrix, (0, 2, 3, 1))


def couplings(key, tag, sign, column):
    dmat, unused = diag_pair(key)
    rho, tau = decay(key, tag)
    count = layout_ints(key)[2][:, column]
    random_keys = jax.random.split(jax.random.fold_in(key, tag + 5), 4)
    two = (count == 2)[:, None]
    weight_one = jnp.where(two, jax.random.uniform(random_keys[0], (BLOCK_TOTAL, NCELL), minval=0.5, maxval=0.8), 1.0)
    weight_two = jnp.where(two, 1.0 - weight_one, jax.random.uniform(random_keys[1], (BLOCK_TOTAL, NCELL), minval=0.2, maxval=0.5))
    result = []
    for slot, weight in enumerate([weight_one, weight_two]):
        jitter = 0.015 * jax.random.normal(random_keys[2 + slot], (BLOCK_TOTAL, NCELL, 5, 5))
        target = sign * (weight * rho)[:, :, None, None] * (jnp.eye(5, dtype=jnp.float32) + jitter)
        result.append(to_layout(jnp.matmul(dmat, target, precision=lax.Precision.HIGHEST)))
    return jnp.stack(result, 1).astype(jnp.float32)


def draw_rhs(key, part):
    random_keys = jax.random.split(jax.random.fold_in(key, 41), 1)
    rows = jnp.arange(BLOCK_TOTAL, dtype=jnp.float32)
    cells = jnp.arange(NCELL, dtype=jnp.float32)
    ramp = (1.0 + 2.0 * rows / max(BLOCK_TOTAL - 1, 1))[:, None, None, None] * (1.0 + 0.5 * cells / max(NCELL - 1, 1))[None, None, None, :]
    values = jnp.clip(jax.random.normal(random_keys[0], (BLOCK_TOTAL, VARS, RHS, NCELL)), -6.0, 6.0) * ramp
    return values.astype(jnp.float32)


def draw_diag_block(key, part):
    dmat, dinv = diag_pair(key)
    return to_layout(dmat).astype(jnp.float32)


def draw_diag_inverse(key, part):
    dmat, dinv = diag_pair(key)
    return to_layout(dinv).astype(jnp.float32)


def draw_lower_coef(key, part):
    return couplings(key, 21, -1.0, 0)


def draw_upper_coef(key, part):
    return couplings(key, 31, 1.0, 1)


def draw_side_coef(key, part):
    dmat, unused = diag_pair(key)
    random_keys = jax.random.split(jax.random.fold_in(key, 51), 2)
    result = []
    for side in range(2):
        target = 0.2 * jax.random.normal(random_keys[side], (BLOCK_TOTAL, NCELL, 5, 5))
        result.append(to_layout(jnp.matmul(dmat, target, precision=lax.Precision.HIGHEST)))
    return jnp.stack(result, 1).astype(jnp.float32)


def draw_lower_cols(key, part):
    low_off, up_off, count = layout_ints(key)
    rows = jnp.arange(BLOCK_TOTAL, dtype=jnp.int32)
    return (rows[:, None] - low_off).astype(jnp.int32)


def draw_upper_cols(key, part):
    low_off, up_off, count = layout_ints(key)
    rows = jnp.arange(BLOCK_TOTAL, dtype=jnp.int32)
    return (rows[:, None] + up_off).astype(jnp.int32)


def draw_counts(key, part):
    low_off, up_off, count = layout_ints(key)
    return count


def setup_inputs(seed: int = 0) -> dict:
    splits = jax.random.split(jax.random.key(seed), 10)
    return {
        "rhs": draw_rhs(jax.random.fold_in(splits[9], 71), 0),
        "diag_block": draw_diag_block(jax.random.fold_in(splits[9], 71), 0),
        "diag_inverse": draw_diag_inverse(jax.random.fold_in(splits[9], 71), 0),
        "lower_coef": draw_lower_coef(jax.random.fold_in(splits[9], 71), 0),
        "upper_coef": draw_upper_coef(jax.random.fold_in(splits[9], 71), 0),
        "side_coef": draw_side_coef(jax.random.fold_in(splits[9], 71), 0),
        "lower_cols": draw_lower_cols(jax.random.fold_in(splits[9], 71), 0),
        "upper_cols": draw_upper_cols(jax.random.fold_in(splits[9], 71), 0),
        "counts": draw_counts(jax.random.fold_in(splits[9], 71), 0),
    }


def mat_apply(matrix, vector):
    return jnp.einsum('ijc,jqc->iqc', matrix, vector, precision=lax.Precision.HIGHEST)

def sweep_all(coef, inverse, source, offsets, active, forward):
    start = jnp.zeros((REACH,) + source.shape[1:], jnp.float32)

    def step(window, item):
        mats, inv, src, off, act = item
        acc = jnp.zeros_like(src)
        for slot in range(SLOTS):
            near = lax.dynamic_index_in_dim(window, (off[slot] - 1).astype(jnp.int32), 0, keepdims=False)
            acc = acc + act[slot] * mat_apply(mats[slot], near)
        if forward:
            out = mat_apply(inv, src - acc)
        else:
            out = src - mat_apply(inv, acc)
        return (jnp.concatenate([out[None], window[:-1]], 0), out)
    _, outs = lax.scan(step, start, (coef, inverse, source, offsets, active), reverse=not forward)
    return outs

def reference(rhs, diag_block, diag_inverse, lower_coef, upper_coef, side_coef, lower_cols, upper_cols, counts):
    rows = jnp.arange(rhs.shape[0], dtype=jnp.int32)
    slot_ids = jnp.arange(SLOTS, dtype=jnp.int32)
    lower_off = (rows[:, None] - lower_cols).astype(jnp.int32)
    upper_off = (upper_cols - rows[:, None]).astype(jnp.int32)
    act_low = (slot_ids[None, :] < counts[:, 0:1]).astype(jnp.float32)
    act_up = (slot_ids[None, :] < counts[:, 1:2]).astype(jnp.float32)
    ysweep = sweep_all(lower_coef, diag_inverse, rhs, lower_off, act_low, True)
    correction = sweep_all(upper_coef, diag_inverse, ysweep, upper_off, act_up, False)
    hi = lax.Precision.HIGHEST
    image = jnp.einsum('bijc,bjqc->biqc', diag_block, correction, precision=hi)
    padded = jnp.pad(correction, ((REACH, REACH), (0, 0), (0, 0), (0, 0)))
    for slot in range(SLOTS):
        near = padded[(lower_cols[:, slot] + REACH).astype(jnp.int32)]
        image = image + act_low[:, slot, None, None, None] * jnp.einsum('bijc,bjqc->biqc', lower_coef[:, slot], near, precision=hi)
        near = padded[(upper_cols[:, slot] + REACH).astype(jnp.int32)]
        image = image + act_up[:, slot, None, None, None] * jnp.einsum('bijc,bjqc->biqc', upper_coef[:, slot], near, precision=hi)
    zeros = jnp.zeros(correction.shape[:3] + (1,), jnp.float32)
    west = jnp.concatenate([zeros, correction[..., :-1]], 3)
    east = jnp.concatenate([correction[..., 1:], zeros], 3)
    image = image + jnp.einsum('bijc,bjqc->biqc', side_coef[:, 0], west, precision=hi)
    image = image + jnp.einsum('bijc,bjqc->biqc', side_coef[:, 1], east, precision=hi)
    resid = rhs - image
    msq = lax.optimization_barrier(jnp.mean(resid * resid, axis=(0, 1, 3)))
    residual_unit = resid / jnp.sqrt(msq + 1e-06)[None, None, :, None]
    return (correction, residual_unit)
```

```python
import functools

import jax
import jax.numpy as jnp
from jax import lax
from jax.experimental import pallas as pl
from jax.experimental.pallas import tpu as pltpu
from jax.sharding import PartitionSpec as P

VARS = 5
RHS = 8
REACH = 3
SLOTS = 2
STATE = REACH * VARS
LANES = 128
PAIR = VARS * VARS * SLOTS
FWIDE = 24
BWIDE = 40
FROWS = STATE * FWIDE
OUT_TILES = 8
BACK_TILES = 2
F32 = jnp.float32
VMEM = pltpu.VMEM
MESH = pl.DeviceIdType.MESH


def row(ref, *index):
    *lead, at = index
    return ref[(*lead, pl.ds(at, RHS, stride=0), slice(None))]


def lanes_of(shape):
    return lax.broadcasted_iota(jnp.int32, shape, len(shape) - 1)


def chunk(t):
    return slice(8 * t, 8 * t + 8)


def near(cols, counts, side, slot, b, start, forward, absent):
    col = cols[slot, b] - start
    used = slot < counts[side, b]
    return jnp.where(used, col + REACH if forward else col, absent)


def local_kernel(blocks, lcol, ucol, counts, rhs, dinv, low, up, send, z, aup, alow, y, vals):
    start = lax.axis_index("chain") * blocks
    absent = blocks + REACH

    for coef, out in ((low, alow), (up, aup)):
        for group in range(blocks // 8):
            rows = pl.ds(8 * group, 8)
            inv = [dinv[q, rows, :] for q in range(VARS * VARS)]
            for slot in range(SLOTS):
                for j in range(VARS):
                    col = [
                        coef[pl.ds(8 * group * PAIR + (m * VARS + j) * SLOTS + slot, 8, stride=PAIR), :]
                        for m in range(VARS)
                    ]
                    for i in range(VARS):
                        acc = inv[i * VARS] * col[0]
                        for m in range(1, VARS):
                            acc = acc + inv[i * VARS + m] * col[m]
                        out[slot * 25 + i * VARS + j, rows, :] = acc

    fsub = lax.broadcasted_iota(jnp.int32, (FWIDE, LANES), 0)
    bsub = lax.broadcasted_iota(jnp.int32, (BWIDE, LANES), 0)
    for d in range(1, REACH + 1):
        for v in range(VARS):
            q = (d - 1) * VARS + v
            y[REACH - d, v] = jnp.where(fsub == RHS + q, 1.0, 0.0).astype(F32)
            z[blocks - 1 + d, v] = jnp.where(bsub == FWIDE + q, 1.0, 0.0).astype(F32)
    for v in range(VARS):
        y[absent, v] = jnp.zeros((FWIDE, LANES), F32)
        z[absent, v] = jnp.zeros((BWIDE, LANES), F32)

    def forward(b, carry):
        at = [near(lcol, counts, 0, k, b, start, True, absent) for k in range(SLOTS)]
        e = [
            [[y[at[k], j, chunk(t), :] for t in range(3)] for j in range(VARS)]
            for k in range(SLOTS)
        ]
        src = [rhs[b, m] for m in range(VARS)]
        for i in range(VARS):
            w = row(dinv, i * VARS, b) * src[0]
            for m in range(1, VARS):
                w = w + row(dinv, i * VARS + m, b) * src[m]
            part = []
            for k in range(SLOTS):
                acc = None
                for j in range(VARS):
                    c = row(alow, k * 25 + i * VARS + j, b)
                    new = [c * e[k][j][t] for t in range(3)]
                    acc = new if acc is None else [p + q for p, q in zip(acc, new)]
                part.append(acc)
            for t in range(3):
                total = part[0][t] + part[1][t]
                y[b + REACH, i, chunk(t), :] = w - total if t == 0 else -total
        return carry

    lax.fori_loop(0, blocks, forward, 0)

    def backward(step, carry):
        b = blocks - 1 - step
        at = [near(ucol, counts, 1, k, b, start, False, absent) for k in range(SLOTS)]
        for group in ((0, 1, 2), (3, 4)):
            e = [
                [[z[at[k], j, chunk(t), :] for t in group] for j in range(VARS)]
                for k in range(SLOTS)
            ]
            for i in range(VARS):
                part = []
                for k in range(SLOTS):
                    acc = None
                    for j in range(VARS):
                        c = row(aup, k * 25 + i * VARS + j, b)
                        new = [c * x for x in e[k][j]]
                        acc = new if acc is None else [p + q for p, q in zip(acc, new)]
                    part.append(acc)
                for n, t in enumerate(group):
                    total = part[0][n] + part[1][n]
                    z[b, i, chunk(t), :] = y[b + REACH, i, chunk(t), :] - total if t < 3 else -total
        return carry

    lax.fori_loop(0, blocks, backward, 0)

    for d in range(1, REACH + 1):
        for v in range(VARS):
            q = (d - 1) * VARS + v
            vals[q * FWIDE : (q + 1) * FWIDE, :] = y[REACH + blocks - d, v]
            vals[FROWS + q * BWIDE : FROWS + (q + 1) * BWIDE, :] = z[d - 1, v]
    used = FROWS + STATE * BWIDE
    vals[used:, :] = jnp.zeros((OUT_TILES * LANES - used, LANES), F32)
    half = LANES // 2
    for tile in range(OUT_TILES):
        turned = vals[tile * LANES : (tile + 1) * LANES, :].T
        for c in range(2):
            for first in range(0, half, 8):
                at = (first * 2 + c) * OUT_TILES + tile
                send[pl.ds(at, 8, stride=2 * OUT_TILES), :] = turned[c * half + first : c * half + first + 8]


def exchange_kernel(nodes, src, dst, send_sem, recv_sem, own_sem):
    me = lax.axis_index("chain")
    barrier = pltpu.get_barrier_semaphore()

    def greet(k, carry):
        pl.semaphore_signal(
            barrier, inc=1, device_id={"chain": lax.rem(me + k, nodes)}, device_id_type=MESH
        )
        return carry

    lax.fori_loop(1, nodes, greet, 0)
    own = pltpu.make_async_copy(src.at[me], dst.at[me], own_sem)
    own.start()
    pl.semaphore_wait(barrier, nodes - 1)

    def post(k, carry):
        to = lax.rem(me + k, nodes)
        pltpu.make_async_remote_copy(
            src_ref=src.at[to],
            dst_ref=dst.at[me],
            send_sem=send_sem,
            recv_sem=recv_sem,
            device_id={"chain": to},
            device_id_type=MESH,
        ).start()
        return carry

    lax.fori_loop(1, nodes, post, 0)
    own.wait()
    pltpu.make_async_remote_copy(
        src_ref=src.at[pl.ds(0, nodes - 1)],
        dst_ref=dst.at[pl.ds(0, nodes - 1)],
        send_sem=send_sem,
        recv_sem=recv_sem,
        device_id={"chain": lax.rem(me + 1, nodes)},
        device_id_type=MESH,
    ).wait()


def exchange(x, nodes, collective_id):
    x = x.reshape(nodes, x.shape[0] // nodes, LANES)
    out = pl.pallas_call(
        functools.partial(exchange_kernel, nodes),
        out_shape=jax.ShapeDtypeStruct(x.shape, x.dtype),
        in_specs=[pl.BlockSpec(memory_space=pl.ANY)],
        out_specs=pl.BlockSpec(memory_space=pl.ANY),
        scratch_shapes=[pltpu.SemaphoreType.DMA] * 3,
        compiler_params=pltpu.CompilerParams(collective_id=collective_id, has_side_effects=True),
        name=f"exchange{collective_id}",
    )(x)
    return out.reshape(x.shape[0] * x.shape[1], LANES)


def scan(read, write, lane, span, ahead):
    shift = 1
    while shift < span:
        last = 2 * shift >= span
        turn = LANES - shift if ahead else shift
        inside = lane < span - shift if ahead else lane >= shift
        old = [[read(i, t) for t in range(3)] for i in range(STATE)]
        new = []
        for t in range(1 if last else 3):
            e = [pltpu.roll(old[j][t], turn, 1) for j in range(STATE)]
            fresh = []
            for i in range(STATE):
                acc = old[i][0] if t == 0 else None
                for j in range(STATE):
                    term = write.coef(i, j) * e[j]
                    acc = term if acc is None else acc + term
                fresh.append(jnp.where(inside, acc, old[i][t]))
            new.append(fresh)
        write.store(new)
        shift *= 2


class Maps:
    def __init__(self, front, back):
        self.front, self.back = front, back

    def read(self, i, t):
        return self.front[i, chunk(t), :]

    def coef(self, i, j):
        return row(self.front, i, RHS + j)

    def store(self, new):
        for t, column in enumerate(new):
            for i, value in enumerate(column):
                self.back[i, chunk(t), :] = value
        self.front, self.back = self.back, self.front


def chain_kernel(nodes, recv, back, vals, m0, m1):
    half = LANES // 2
    for tile in range(OUT_TILES):
        both = [recv[pl.ds(c * OUT_TILES + tile, half, stride=2 * OUT_TILES), :] for c in range(2)]
        vals[tile * LANES : (tile + 1) * LANES, :] = jnp.concatenate(both, 0).T
    lane = lax.rem(lanes_of((8, LANES)), nodes)

    for i in range(STATE):
        m0[i] = vals[i * FWIDE : (i + 1) * FWIDE, :]
    maps = Maps(m0, m1)
    scan(maps.read, maps, lane, nodes, False)
    entering = [
        jnp.where(lane == 0, 0.0, pltpu.roll(maps.read(i, 0), 1, 1)) for i in range(STATE)
    ]

    for i in range(STATE):
        at = FROWS + i * BWIDE
        acc = vals[at : at + 8, :]
        for j in range(STATE):
            acc = acc + row(vals, at + RHS + j) * entering[j]
        m0[i, chunk(0), :] = acc
        m0[i, 8:24, :] = vals[at + FWIDE : at + BWIDE, :]
    maps = Maps(m0, m1)
    scan(maps.read, maps, lane, nodes, True)
    following = [
        jnp.where(lane == nodes - 1, 0.0, pltpu.roll(maps.read(i, 0), LANES - 1, 1))
        for i in range(STATE)
    ]

    for tile, state in enumerate((entering, following)):
        turned = jnp.concatenate(state + [jnp.zeros((8, LANES), F32)], 0).T
        for c in range(2):
            for first in range(0, half, 8):
                at = (first * 2 + c) * BACK_TILES + tile
                back[pl.ds(at, 8, stride=2 * BACK_TILES), :] = turned[c * half + first : c * half + first + 8]


def correct_kernel(blocks, ucol, counts, back, z, aup, corr, u, edges, padded):
    start = lax.axis_index("chain") * blocks
    absent = blocks + REACH
    half = LANES // 2
    state = []
    for tile in range(BACK_TILES):
        both = [back[pl.ds(c * BACK_TILES + tile, half, stride=2 * BACK_TILES), :] for c in range(2)]
        turned = jnp.concatenate(both, 0).T
        state.append([turned[8 * q : 8 * q + 8] for q in range(STATE)])
    entering, following = state
    for d in range(1, REACH + 1):
        for v in range(VARS):
            padded[blocks - 1 + d, v] = following[(d - 1) * VARS + v]
    for v in range(VARS):
        padded[absent, v] = jnp.zeros((RHS, LANES), F32)
    lane = lanes_of((RHS, LANES))

    def solve(b, carry):
        head, tail = carry
        for i in range(VARS):
            acc = [z[b, i, chunk(0), :], None]
            for n, (offset, values) in enumerate(((RHS, entering), (FWIDE, following))):
                for j in range(STATE):
                    term = row(z, b, i, offset + j) * values[j]
                    acc[n] = term if acc[n] is None else acc[n] + term
            value = acc[0] + acc[1]
            corr[b, i] = value
            padded[b, i] = value
            here = lane == b * VARS + i
            head = jnp.where(here, value[:, 0:1], head)
            tail = jnp.where(here, value[:, LANES - 1 :], tail)
        return head, tail

    none = jnp.zeros((RHS, LANES), F32)
    head, tail = lax.fori_loop(0, blocks, solve, (none, none))
    edges[0] = head
    edges[1] = tail

    def couple(b, carry):
        at = [near(ucol, counts, 1, k, b, start, False, absent) for k in range(SLOTS)]
        e = [[padded[at[k], j] for j in range(VARS)] for k in range(SLOTS)]
        for i in range(VARS):
            part = []
            for k in range(SLOTS):
                acc = row(aup, k * 25 + i * VARS, b) * e[k][0]
                for j in range(1, VARS):
                    acc = acc + row(aup, k * 25 + i * VARS + j, b) * e[k][j]
                part.append(acc)
            u[b, i] = part[0] + part[1]
        return carry

    lax.fori_loop(0, blocks, couple, 0)


def halo_kernel(nodes, subs, blocks, u, edges, before, beside, send_sem, recv_sem):
    me, sub = lax.axis_index("chain"), lax.axis_index("sub")
    left, right = lax.rem(sub + subs - 1, subs), lax.rem(sub + 1, subs)
    later, earlier = lax.rem(me + 1, nodes), lax.rem(me + nodes - 1, nodes)
    barrier = pltpu.get_barrier_semaphore()
    for peer in ({"sub": left}, {"sub": right}, {"chain": later}, {"chain": earlier}):
        pl.semaphore_signal(barrier, inc=1, device_id=peer, device_id_type=MESH)
    pl.semaphore_wait(barrier, 4)
    plan = (
        (u.at[pl.ds(blocks - REACH, REACH)], before, {"chain": later}),
        (edges.at[1], beside.at[0], {"sub": right}),
        (edges.at[0], beside.at[1], {"sub": left}),
    )
    copies = [
        pltpu.make_async_remote_copy(
            src_ref=src,
            dst_ref=dst,
            send_sem=send_sem.at[n],
            recv_sem=recv_sem.at[n],
            device_id=peer,
            device_id_type=MESH,
        )
        for n, (src, dst, peer) in enumerate(plan)
    ]
    for copy in copies:
        copy.start()
    for copy in copies:
        copy.wait()


def resid_kernel(blocks, subs, lcol, counts, low, side, corr, u, before, beside, resid, part, padded):
    me, sub = lax.axis_index("chain"), lax.axis_index("sub")
    start = me * blocks
    absent = blocks + REACH
    for d in range(REACH):
        for v in range(VARS):
            padded[d, v] = jnp.where(me == 0, 0.0, before[d, v])
    for v in range(VARS):
        padded[absent, v] = jnp.zeros((RHS, LANES), F32)

    def fill(b, carry):
        for v in range(VARS):
            padded[b + REACH, v] = u[b, v]
        return carry

    lax.fori_loop(0, blocks, fill, 0)
    lane = lanes_of((RHS, LANES))
    west_edge = jnp.where(sub == 0, 0.0, beside[0])
    east_edge = jnp.where(sub == subs - 1, 0.0, beside[1])

    def body(b, square):
        at = [near(lcol, counts, 0, k, b, start, True, absent) for k in range(SLOTS)]
        e = [[padded[at[k], j] for j in range(VARS)] for k in range(SLOTS)]
        west, east = [], []
        for j in range(VARS):
            value, k = corr[b, j], b * VARS + j
            west.append(
                jnp.where(
                    lane == 0,
                    pltpu.roll(west_edge, lax.rem(LANES - k, LANES), 1),
                    pltpu.roll(value, 1, 1),
                )
            )
            east.append(
                jnp.where(
                    lane == LANES - 1,
                    pltpu.roll(east_edge, LANES - 1 - k, 1),
                    pltpu.roll(value, LANES - 1, 1),
                )
            )
        for i in range(VARS):
            total = None
            for sign, coef, k, values in (
                (1, low, 0, e[0]),
                (1, low, 1, e[1]),
                (-1, side, 0, west),
                (-1, side, 1, east),
            ):
                acc = None
                for j in range(VARS):
                    term = row(coef, b * PAIR + (i * VARS + j) * SLOTS + k) * values[j]
                    acc = term if acc is None else acc + term
                total = acc if total is None else total + acc if sign > 0 else total - acc
            resid[b, i] = total
            square = square + total * total
        return square

    square = lax.fori_loop(0, blocks, body, jnp.zeros((RHS, LANES), F32))
    sums = jnp.sum(square, axis=1, keepdims=True)
    diagonal = lax.broadcasted_iota(jnp.int32, (RHS, LANES), 0) == lane
    part[...] = jnp.sum(jnp.where(diagonal, sums, 0.0), axis=0, keepdims=True)


def total_kernel(nodes, subs, part, out, wide, stage, deep, send_sem, recv_sem, own_sem):
    me, sub = lax.axis_index("chain"), lax.axis_index("sub")
    barrier = pltpu.get_barrier_semaphore()
    groups = (("chain", me, nodes), ("sub", sub, subs))
    for axis, index, count in groups:

        def greet(k, carry, axis=axis, index=index, count=count):
            pl.semaphore_signal(
                barrier, inc=1, device_id={axis: lax.rem(index + k, count)}, device_id_type=MESH
            )
            return carry

        lax.fori_loop(1, count, greet, 0)
    pl.semaphore_wait(barrier, nodes + subs - 2)
    for n, ((axis, index, count), src, dst) in enumerate(zip(groups, (part, stage), (wide, deep))):

        def copy(to, src=src, dst=dst, axis=axis, index=index, n=n):
            return pltpu.make_async_remote_copy(
                src_ref=src,
                dst_ref=dst.at[index],
                send_sem=send_sem.at[n],
                recv_sem=recv_sem.at[n],
                device_id={axis: to},
                device_id_type=MESH,
            )

        def post(k, carry, copy=copy, index=index, count=count):
            copy(lax.rem(index + k, count)).start()
            return carry

        lax.fori_loop(1, count, post, 0)
        own = pltpu.make_async_copy(src, dst.at[index], own_sem)
        own.start()
        own.wait()
        pltpu.make_async_remote_copy(
            src_ref=dst.at[pl.ds(0, count - 1)],
            dst_ref=dst.at[pl.ds(0, count - 1)],
            send_sem=send_sem.at[n],
            recv_sem=recv_sem.at[n],
            device_id={axis: lax.rem(index + 1, count)},
            device_id_type=MESH,
        ).wait()
        total = jnp.sum(dst[...], axis=0)
        if n == 0:
            stage[...] = total
        else:
            out[...] = total


def scale_kernel(entries, resid, total, out):
    lane = lanes_of((RHS, LANES))
    diagonal = lax.broadcasted_iota(jnp.int32, (RHS, LANES), 0) == lane
    wide = jnp.broadcast_to(total[...], (RHS, LANES))
    sums = jnp.sum(jnp.where(diagonal, wide, 0.0), axis=1, keepdims=True)
    factor = jnp.broadcast_to(lax.rsqrt(sums / entries + 1e-6), (RHS, LANES))
    out[...] = resid[...] * factor[None, None]


def spec(space):
    return pl.BlockSpec(memory_space=space)


def on_device(kernel, name, ints, floats, outs, scratch):
    return pl.pallas_call(
        kernel,
        out_shape=tuple(jax.ShapeDtypeStruct(shape, F32) for shape in outs),
        in_specs=[spec(pltpu.SMEM)] * len(ints) + [spec(VMEM)] * len(floats),
        out_specs=tuple(spec(VMEM) for _ in outs),
        scratch_shapes=[VMEM(shape, F32) for shape in scratch],
        compiler_params=pltpu.CompilerParams(vmem_limit_bytes=40 << 20),
        name=name,
    )(*ints, *floats)


def shards(nodes, subs, rhs, diag_block, diag_inverse, lower_coef, upper_coef, side_coef, lower_cols, upper_cols, counts):
    blocks = rhs.shape[0]
    cells = rhs.shape[3]
    padded = blocks + REACH + 1
    dinv = jnp.transpose(diag_inverse, (1, 2, 0, 3)).reshape(VARS * VARS, blocks, cells)
    low, up, side = (
        jnp.transpose(x, (0, 2, 3, 1, 4)).reshape(blocks * PAIR, cells)
        for x in (lower_coef, upper_coef, side_coef)
    )
    lcol, ucol, cnt = lower_cols.T, upper_cols.T, counts.T
    plane = (blocks, VARS, RHS, cells)
    send, z, aup = on_device(
        functools.partial(local_kernel, blocks),
        "local",
        (lcol, ucol, cnt),
        (rhs, dinv, low, up),
        ((OUT_TILES * cells, cells), (padded, VARS, BWIDE, cells), (PAIR, blocks, cells)),
        ((PAIR, blocks, cells), (padded, VARS, FWIDE, cells), (OUT_TILES * cells, cells)),
    )
    recv = exchange(send, nodes, 0)
    (back,) = on_device(
        functools.partial(chain_kernel, nodes),
        "chain",
        (),
        (recv,),
        ((2 * BACK_TILES * nodes, cells),),
        ((OUT_TILES * cells, cells), (STATE, FWIDE, cells), (STATE, FWIDE, cells)),
    )
    back = exchange(back, nodes, 1)
    corr, u, edges = on_device(
        functools.partial(correct_kernel, blocks),
        "correct",
        (ucol, cnt),
        (back, z, aup),
        (plane, plane, (2, RHS, cells)),
        ((padded, VARS, RHS, cells),),
    )
    before, beside = pl.pallas_call(
        functools.partial(halo_kernel, nodes, subs, blocks),
        out_shape=(
            jax.ShapeDtypeStruct((REACH, VARS, RHS, cells), F32),
            jax.ShapeDtypeStruct((2, RHS, cells), F32),
        ),
        in_specs=[spec(pl.ANY)] * 2,
        out_specs=(spec(pl.ANY), spec(pl.ANY)),
        scratch_shapes=[pltpu.SemaphoreType.DMA((3,)), pltpu.SemaphoreType.DMA((3,))],
        compiler_params=pltpu.CompilerParams(collective_id=2, has_side_effects=True),
        name="halo",
    )(u, edges)
    resid, part = on_device(
        functools.partial(resid_kernel, blocks, subs),
        "resid",
        (lcol, cnt),
        (low, side, corr, u, before, beside),
        (plane, (1, cells)),
        ((padded, VARS, RHS, cells),),
    )
    total = pl.pallas_call(
        functools.partial(total_kernel, nodes, subs),
        out_shape=jax.ShapeDtypeStruct((1, cells), F32),
        in_specs=[spec(VMEM)],
        out_specs=spec(VMEM),
        scratch_shapes=[
            VMEM((nodes, 1, cells), F32),
            VMEM((1, cells), F32),
            VMEM((subs, 1, cells), F32),
            pltpu.SemaphoreType.DMA((2,)),
            pltpu.SemaphoreType.DMA((2,)),
            pltpu.SemaphoreType.DMA,
        ],
        compiler_params=pltpu.CompilerParams(collective_id=3, has_side_effects=True),
        name="total",
    )(part)
    entries = nodes * blocks * VARS * subs * cells
    (unit,) = on_device(
        functools.partial(scale_kernel, entries), "scale", (), (resid, total), (plane,), ()
    )
    return corr, unit


def solution(mesh):
    nodes, subs = mesh.shape["chain"], mesh.shape["sub"]
    plane = P("chain", None, None, "sub")
    coef = P("chain", None, None, None, "sub")
    return jax.shard_map(
        functools.partial(shards, nodes, subs),
        mesh=mesh,
        in_specs=(plane, plane, plane, coef, coef, coef, P("chain", None), P("chain", None), P("chain", None)),
        out_specs=(plane, plane),
        check_vma=False,
    )
```

```python
import functools

import jax
import jax.numpy as jnp
from jax import lax
from jax.experimental import pallas as pl
from jax.experimental.pallas import tpu as pltpu
from jax.sharding import PartitionSpec as P

VARS = 5
RHS = 8
REACH = 3
SLOTS = 2
STATE = REACH * VARS
LANES = 128
PAIR = VARS * VARS * SLOTS
FWIDE = 24
GWIDE = 16
SLOT = 8
FULL, MAP, ONE = 3, 2, 1
F32 = jnp.float32
VMEM = pltpu.VMEM
MESH = pl.DeviceIdType.MESH
VMEM_LIMIT = 61 << 20


def row(ref, *index):
    *lead, at = index
    return ref[(*lead, pl.ds(at, RHS, stride=0), slice(None))]


def lanes_of(shape):
    return lax.broadcasted_iota(jnp.int32, shape, len(shape) - 1)


def chunk(t):
    return slice(8 * t, 8 * t + 8)


def near(cols, counts, side, slot, b, start, forward, absent):
    col = cols[slot, b] - start
    used = slot < counts[side, b]
    return jnp.where(used, col + REACH if forward else col, absent)


def couple(coef, dinv, out, blocks):
    for group in range(blocks // 8):
        rows = pl.ds(8 * group, 8)
        inv = [dinv[q, rows, :] for q in range(VARS * VARS)]
        for slot in range(SLOTS):
            for j in range(VARS):
                col = [
                    coef[pl.ds(8 * group * PAIR + (m * VARS + j) * SLOTS + slot, 8, stride=PAIR), :]
                    for m in range(VARS)
                ]
                for i in range(VARS):
                    acc = inv[i * VARS] * col[0]
                    for m in range(1, VARS):
                        acc = acc + inv[i * VARS + m] * col[m]
                    out[slot * 25 + i * VARS + j, rows, :] = acc


def coupled(coef, b, values, emit):
    for i in range(VARS):
        part = []
        for k in range(SLOTS):
            acc = None
            for j in range(VARS):
                c = row(coef, k * 25 + i * VARS + j, b)
                new = [c * x for x in values[k][j]]
                acc = new if acc is None else [p + q for p, q in zip(acc, new)]
            part.append(acc)
        for t, (p, q) in enumerate(zip(*part)):
            emit(i, t, p + q)


def pack(vals, tiles, send):
    half = LANES // 2
    for tile in range(tiles):
        turned = vals[tile * LANES : (tile + 1) * LANES, :].T
        for c in range(2):
            for first in range(0, half, 8):
                at = first * SLOT + c * tiles + tile
                send[pl.ds(at, 8, stride=SLOT), :] = turned[c * half + first : c * half + first + 8]


def unpack(recv, tiles, vals):
    half = LANES // 2
    for tile in range(tiles):
        both = [recv[pl.ds(c * tiles + tile, half, stride=SLOT), :] for c in range(2)]
        vals[tile * LANES : (tile + 1) * LANES, :] = jnp.concatenate(both, 0).T


def shifts(span):
    return [1 << n for n in range(span.bit_length() - 1)]


def turned(x, shift, ahead):
    return pltpu.roll(x, LANES - shift if ahead else shift, 1)


def scan_maps(stack, lane, span, ahead):
    for n, shift in enumerate(shifts(span)[:-1]):
        inside = lane < span - shift if ahead else lane >= shift
        for t in range(2):
            e = [turned(stack[n, j, chunk(t), :], shift, ahead) for j in range(STATE)]
            for i in range(STATE):
                acc = None
                for j in range(STATE):
                    term = row(stack, n, i, j) * e[j]
                    acc = term if acc is None else acc + term
                stack[n + 1, i, chunk(t), :] = jnp.where(inside, acc, stack[n, i, chunk(t), :])


def scan_states(stack, state, lane, span, ahead):
    for n, shift in enumerate(shifts(span)):
        inside = lane < span - shift if ahead else lane >= shift
        e = [turned(x, shift, ahead) for x in state]
        fresh = []
        for i in range(STATE):
            acc = state[i]
            for j in range(STATE):
                acc = acc + row(stack, n, i, j) * e[j]
            fresh.append(jnp.where(inside, acc, state[i]))
        state = fresh
    edge = lane == span - 1 if ahead else lane == 0
    return [jnp.where(edge, 0.0, turned(x, 1, ahead)) for x in state]


def main_kernel(
    nodes, subs, line, lcol, ucol, counts, rhs_in, dinv_in, low_in, up_in, side_in,
    corr_out, resid_out, total,
    resid, rhs, dinv, low, up, side, alow, aup, y, zb, zm, vals,
    s1, s2, s3, r1, r2, r3, s4, s5, r4, r5, gf, gb,
    zpad, upad, before, edges, beside, part, stage, wide, deep,
    load_sem, send_sem, recv_sem, own_sem, out_sem,
):
    blocks = rhs.shape[0]
    me, sub = lax.axis_index("chain"), lax.axis_index("sub")
    start, absent = me * blocks, blocks + REACH
    loads = [
        pltpu.make_async_copy(src, dst, load_sem.at[n])
        for n, (src, dst) in enumerate(
            ((low_in, low), (dinv_in, dinv), (rhs_in, rhs), (up_in, up), (side_in, side))
        )
    ]
    for load in loads:
        load.start()

    barrier = pltpu.get_barrier_semaphore()
    flat = (me // line) * subs + sub
    place = lax.rem(me, line)

    def cross(k):
        other = lax.rem(flat + k, subs * (nodes // line))
        return {"chain": (other // subs) * line + place, "sub": lax.rem(other, subs)}

    def along(k):
        return {"chain": me - place + lax.rem(place + k, line)}

    def around(k):
        return {"chain": lax.rem(me + k, nodes)}

    across = subs * (nodes // line)
    groups = ((around, nodes), (cross, across))
    for peer, count in groups:

        def greet(k, carry, peer=peer):
            pl.semaphore_signal(barrier, inc=1, device_id=peer(k), device_id_type=MESH)
            return carry

        lax.fori_loop(1, count, greet, 0)

    def remote(src, dst, n, peer):
        return pltpu.make_async_remote_copy(
            src_ref=src,
            dst_ref=dst,
            send_sem=send_sem.at[n],
            recv_sem=recv_sem.at[n],
            device_id=peer,
            device_id_type=MESH,
        )

    mine = pl.multiple_of(me * SLOT, SLOT)

    def own(src, dst, tiles, n):
        rows = pl.ds(mine, 2 * tiles)
        return pltpu.make_async_copy(src.at[rows], dst.at[rows], own_sem.at[n])

    def post(src, dst, tiles, n):
        own(src, dst, tiles, n).start()

        def one(k, carry):
            to = lax.rem(me + k, nodes)
            there = pl.ds(pl.multiple_of(to * SLOT, SLOT), 2 * tiles)
            remote(src.at[there], dst.at[pl.ds(mine, 2 * tiles)], n, {"chain": to}).start()
            return carry

        lax.fori_loop(1, nodes, one, 0)

    def whole(src, dst, tiles, n):
        rows = pl.ds(0, 2 * tiles * (nodes - 1))
        return remote(src.at[rows], dst.at[rows], n, around(1))

    def collect(src, dst, tiles, n):
        own(src, dst, tiles, n).wait()
        whole(src, dst, tiles, n).wait_recv()

    fsub = lax.broadcasted_iota(jnp.int32, (FWIDE, LANES), 0)
    gsub = lax.broadcasted_iota(jnp.int32, (GWIDE, LANES), 0)
    for d in range(1, REACH + 1):
        for v in range(VARS):
            q = (d - 1) * VARS + v
            y[REACH - d, v] = jnp.where(fsub == RHS + q, 1.0, 0.0).astype(F32)
            zb[blocks - 1 + d, v] = jnp.where(gsub == q, 1.0, 0.0).astype(F32)
            zm[blocks - 1 + d, v] = jnp.zeros((FWIDE, LANES), F32)
    none = jnp.zeros((RHS, LANES), F32)
    for v in range(VARS):
        y[absent, v] = jnp.zeros((FWIDE, LANES), F32)
        zm[absent, v] = jnp.zeros((FWIDE, LANES), F32)
        zb[absent, v] = jnp.zeros((GWIDE, LANES), F32)
        zpad[absent, v] = none
        upad[absent, v] = none
    vals[...] = jnp.zeros(vals.shape, F32)

    def lower(b):
        return [near(lcol, counts, 0, k, b, start, True, absent) for k in range(SLOTS)]

    def upper(b):
        return [near(ucol, counts, 1, k, b, start, False, absent) for k in range(SLOTS)]

    def window(ref, at, chunks):
        return [
            [[ref[at[k], j, chunk(t), :] for t in range(chunks)] for j in range(VARS)]
            for k in range(SLOTS)
        ]

    loads[0].wait()
    loads[1].wait()
    couple(low, dinv, alow, blocks)
    loads[2].wait()

    def forward(b, carry):
        values = window(y, lower(b), 3)
        src = [rhs[b, m] for m in range(VARS)]
        own_part = []
        for i in range(VARS):
            w = row(dinv, i * VARS, b) * src[0]
            for m in range(1, VARS):
                w = w + row(dinv, i * VARS + m, b) * src[m]
            own_part.append(w)

        def emit(i, t, value):
            y[b + REACH, i, chunk(t), :] = own_part[i] - value if t == 0 else -value

        coupled(alow, b, values, emit)
        return carry

    lax.fori_loop(0, blocks, forward, 0)
    for d in range(1, REACH + 1):
        for v in range(VARS):
            q = (d - 1) * VARS + v
            vals[q * FWIDE : (q + 1) * FWIDE, :] = y[REACH + blocks - d, v]
    pack(vals, FULL, s1)
    pl.semaphore_wait(barrier, nodes + across - 2)
    post(s1, r1, FULL, 0)

    loads[3].wait()
    couple(up, dinv, aup, blocks)

    def basis(step, carry):
        b = blocks - 1 - step

        def emit(i, t, value):
            zb[b, i, chunk(t), :] = -value

        coupled(aup, b, window(zb, upper(b), 2), emit)
        return carry

    lax.fori_loop(0, blocks, basis, 0)
    for d in range(1, REACH + 1):
        for v in range(VARS):
            q = (d - 1) * VARS + v
            vals[q * GWIDE : (q + 1) * GWIDE, :] = zb[d - 1, v]
    pack(vals, MAP, s2)
    post(s2, r2, MAP, 1)

    def backward(step, carry):
        b = blocks - 1 - step

        def emit(i, t, value):
            zm[b, i, chunk(t), :] = y[b + REACH, i, chunk(t), :] - value

        coupled(aup, b, window(zm, upper(b), 3), emit)
        return carry

    lax.fori_loop(0, blocks, backward, 0)
    for d in range(1, REACH + 1):
        for v in range(VARS):
            q = (d - 1) * VARS + v
            vals[q * FWIDE : (q + 1) * FWIDE, :] = zm[d - 1, v]
    pack(vals, FULL, s3)
    post(s3, r3, FULL, 2)

    lane = lanes_of((RHS, LANES))
    at = lax.rem(lane, nodes)
    collect(s1, r1, FULL, 0)
    unpack(r1, FULL, vals)
    for i in range(STATE):
        gf[0, i] = vals[i * FWIDE + RHS : (i + 1) * FWIDE, :]
    scan_maps(gf, at, nodes, False)
    entering = scan_states(
        gf, [vals[i * FWIDE : i * FWIDE + RHS, :] for i in range(STATE)], at, nodes, False
    )
    vals[STATE * RHS : LANES, :] = none
    for i in range(STATE):
        vals[i * RHS : (i + 1) * RHS, :] = entering[i]
    pack(vals, ONE, s4)
    post(s4, r4, ONE, 3)

    collect(s2, r2, MAP, 1)
    unpack(r2, MAP, vals)
    for i in range(STATE):
        gb[0, i] = vals[i * GWIDE : (i + 1) * GWIDE, :]
    scan_maps(gb, at, nodes, True)
    collect(s3, r3, FULL, 2)
    unpack(r3, FULL, vals)
    state = []
    for i in range(STATE):
        acc = vals[i * FWIDE : i * FWIDE + RHS, :]
        for j in range(STATE):
            acc = acc + row(vals, i * FWIDE + RHS + j) * entering[j]
        state.append(acc)
    following = scan_states(gb, state, at, nodes, True)
    vals[STATE * RHS : LANES, :] = none
    for i in range(STATE):
        vals[i * RHS : (i + 1) * RHS, :] = following[i]
    pack(vals, ONE, s5)
    post(s5, r5, ONE, 4)

    collect(s4, r4, ONE, 3)
    unpack(r4, ONE, vals)
    entering = [vals[i * RHS : (i + 1) * RHS, :] for i in range(STATE)]

    def enter(b, carry):
        for i in range(VARS):
            acc = zm[b, i, chunk(0), :]
            for j in range(STATE):
                acc = acc + row(zm, b, i, RHS + j) * entering[j]
            zpad[b, i] = acc
        return carry

    lax.fori_loop(0, blocks, enter, 0)
    collect(s5, r5, ONE, 4)
    unpack(r5, ONE, vals)
    following = [vals[i * RHS : (i + 1) * RHS, :] for i in range(STATE)]
    for d in range(1, REACH + 1):
        for v in range(VARS):
            zpad[blocks - 1 + d, v] = following[(d - 1) * VARS + v]

    def follow(b, carry):
        head, tail = carry
        for i in range(VARS):
            acc = zpad[b, i]
            for j in range(STATE):
                acc = acc + row(zb, b, i, j) * following[j]
            zpad[b, i] = acc
            here = lane == b * VARS + i
            head = jnp.where(here, acc[:, 0:1], head)
            tail = jnp.where(here, acc[:, LANES - 1 :], tail)
        return head, tail

    head, tail = lax.fori_loop(0, blocks, follow, (none, none))
    edges[0] = head
    edges[1] = tail
    left, right = lax.rem(sub + subs - 1, subs), lax.rem(sub + 1, subs)
    halo = [
        remote(edges.at[1], beside.at[0], 5, {"sub": right}),
        remote(edges.at[0], beside.at[1], 6, {"sub": left}),
        remote(upad.at[pl.ds(blocks, REACH)], before, 7, around(1)),
    ]
    halo[0].start()
    halo[1].start()
    store_corr = pltpu.make_async_copy(zpad.at[pl.ds(0, blocks)], corr_out, out_sem.at[0])
    store_corr.start()

    def difference(step, carry):
        b = blocks - 1 - step

        def emit(i, t, value):
            upad[b + REACH, i] = value

        at = upper(b)
        values = [[[zpad[at[k], j]] for j in range(VARS)] for k in range(SLOTS)]
        coupled(aup, b, values, emit)
        return carry

    lax.fori_loop(0, REACH, difference, 0)
    halo[2].start()
    lax.fori_loop(REACH, blocks, difference, 0)

    def apply(coef, b, i, values):
        total = None
        for k, column in enumerate(values):
            acc = None
            for j in range(VARS):
                term = row(coef, b * PAIR + (i * VARS + j) * SLOTS + k) * column[j]
                acc = term if acc is None else acc + term
            total = acc if total is None else total + acc
        return total

    def before_part(b, carry):
        at = lower(b)
        values = [[upad[at[k], j] for j in range(VARS)] for k in range(SLOTS)]
        for i in range(VARS):
            resid[b, i] = apply(low, b, i, values)
        return carry

    lax.fori_loop(REACH, blocks, before_part, 0)
    halo[2].wait_recv()
    for d in range(REACH):
        for v in range(VARS):
            upad[d, v] = jnp.where(me == 0, 0.0, before[d, v])
    lax.fori_loop(0, REACH, before_part, 0)
    loads[4].wait()
    halo[0].wait_recv()
    halo[1].wait_recv()
    west_edge = jnp.where(sub == 0, 0.0, beside[0])
    east_edge = jnp.where(sub == subs - 1, 0.0, beside[1])

    def side_part(b, square):
        west, east = [], []
        for j in range(VARS):
            value, k = zpad[b, j], b * VARS + j
            west.append(
                jnp.where(
                    lane == 0,
                    pltpu.roll(west_edge, lax.rem(LANES - k, LANES), 1),
                    pltpu.roll(value, 1, 1),
                )
            )
            east.append(
                jnp.where(
                    lane == LANES - 1,
                    pltpu.roll(east_edge, LANES - 1 - k, 1),
                    pltpu.roll(value, LANES - 1, 1),
                )
            )
        for i in range(VARS):
            value = resid[b, i] - apply(side, b, i, (west, east))
            resid[b, i] = value
            square = square + value * value
        return square

    square = lax.fori_loop(0, blocks, side_part, none)
    store_resid = pltpu.make_async_copy(resid, resid_out, out_sem.at[1])
    store_resid.start()
    sums = jnp.sum(square, axis=1, keepdims=True)
    diagonal = lax.broadcasted_iota(jnp.int32, (RHS, LANES), 0) == lane
    part[...] = jnp.sum(jnp.where(diagonal, sums, 0.0), axis=0, keepdims=True)

    rounds = ((along, line, place, part, wide, stage), (cross, across, flat, stage, deep, total))
    for n, (peer, count, index, src, dst, out) in enumerate(rounds):

        def tell(k, carry, peer=peer, src=src, dst=dst, index=index, n=n):
            remote(src, dst.at[index], 8 + n, peer(k)).start()
            return carry

        lax.fori_loop(1, count, tell, 0)
        mine_too = pltpu.make_async_copy(src, dst.at[index], own_sem.at[5 + n])
        mine_too.start()
        mine_too.wait()
        rows = pl.ds(0, count - 1)
        remote(dst.at[rows], dst.at[rows], 8 + n, peer(1)).wait_recv()
        out[...] = jnp.sum(dst[...], axis=0)

    store_corr.wait()
    store_resid.wait()
    for src, dst, tiles, n in (
        (s1, r1, FULL, 0), (s2, r2, MAP, 1), (s3, r3, FULL, 2), (s4, r4, ONE, 3), (s5, r5, ONE, 4)
    ):
        whole(src, dst, tiles, n).wait_send()
    for copy in halo:
        copy.wait_send()
    for n, (peer, count, _, _, dst, _) in enumerate(rounds):
        rows = pl.ds(0, count - 1)
        remote(dst.at[rows], dst.at[rows], 8 + n, peer(1)).wait_send()


def scale_kernel(entries, corr, resid, total, corr_out, out):
    lane = lanes_of((RHS, LANES))
    diagonal = lax.broadcasted_iota(jnp.int32, (RHS, LANES), 0) == lane
    wide = jnp.broadcast_to(total[...], (RHS, LANES))
    sums = jnp.sum(jnp.where(diagonal, wide, 0.0), axis=1, keepdims=True)
    factor = jnp.broadcast_to(lax.rsqrt(sums / entries + 1e-6), (RHS, LANES))
    out[...] = resid[...] * factor[None, None]
    corr_out[...] = corr[...]


def spec(space):
    return pl.BlockSpec(memory_space=space)


def shards(nodes, subs, line, rhs, diag_block, diag_inverse, lower_coef, upper_coef, side_coef, lower_cols, upper_cols, counts):
    blocks = rhs.shape[0]
    cells = rhs.shape[3]
    padded = blocks + REACH + 1
    across = subs * (nodes // line)
    dinv = jnp.transpose(diag_inverse, (1, 2, 0, 3)).reshape(VARS * VARS, blocks, cells)
    low, up, side = (
        jnp.transpose(x, (0, 2, 3, 1, 4)).reshape(blocks * PAIR, cells)
        for x in (lower_coef, upper_coef, side_coef)
    )
    plane = jax.ShapeDtypeStruct((blocks, VARS, RHS, cells), F32)
    slots = VMEM((nodes * SLOT, cells), F32)
    window = VMEM((padded, VARS, RHS, cells), F32)
    depth = len(shifts(nodes))
    corr, resid, total = pl.pallas_call(
        functools.partial(main_kernel, nodes, subs, line),
        out_shape=(plane, plane, jax.ShapeDtypeStruct((1, cells), F32)),
        in_specs=[spec(pltpu.SMEM)] * 3 + [spec(pl.ANY)] * 5,
        out_specs=(spec(pl.ANY), spec(pl.ANY), spec(VMEM)),
        scratch_shapes=[VMEM(plane.shape, F32)]
        + [VMEM(x.shape, F32) for x in (rhs, dinv, low, up, side)]
        + [VMEM((PAIR, blocks, cells), F32)] * 2
        + [VMEM((padded, VARS, wide, cells), F32) for wide in (FWIDE, GWIDE, FWIDE)]
        + [VMEM((FULL * LANES, cells), F32)]
        + [slots] * 10
        + [VMEM((depth, STATE, GWIDE, cells), F32)] * 2
        + [window] * 2
        + [VMEM((REACH, VARS, RHS, cells), F32)]
        + [VMEM((2, RHS, cells), F32)] * 2
        + [VMEM((1, cells), F32)] * 2
        + [VMEM((line, 1, cells), F32), VMEM((across, 1, cells), F32)]
        + [pltpu.SemaphoreType.DMA((n,)) for n in (5, 10, 10, 7, 2)],
        compiler_params=pltpu.CompilerParams(
            collective_id=0, has_side_effects=True, vmem_limit_bytes=VMEM_LIMIT
        ),
        name="sweeps",
    )(lower_cols.T, upper_cols.T, counts.T, rhs, dinv, low, up, side)
    slab = pl.BlockSpec((8, VARS, RHS, cells), lambda n: (n, 0, 0, 0))
    entries = nodes * blocks * VARS * subs * cells
    return pl.pallas_call(
        functools.partial(scale_kernel, entries),
        out_shape=(plane, plane),
        grid=(blocks // 8,),
        in_specs=[slab, slab, pl.BlockSpec((1, cells), lambda n: (0, 0))],
        out_specs=(slab, slab),
        compiler_params=pltpu.CompilerParams(vmem_limit_bytes=VMEM_LIMIT),
        name="scale",
    )(corr, resid, total)


def solution(mesh):
    nodes, subs = mesh.shape["chain"], mesh.shape["sub"]
    line = 16 if nodes % 16 == 0 else nodes
    plane = P("chain", None, None, "sub")
    coef = P("chain", None, None, None, "sub")
    return jax.shard_map(
        functools.partial(shards, nodes, subs, line),
        mesh=mesh,
        in_specs=(plane, plane, plane, coef, coef, coef, P("chain", None), P("chain", None), P("chain", None)),
        out_specs=(plane, plane),
        check_vma=False,
    )
```

```python
import functools

import jax
import jax.numpy as jnp
from jax import lax
from jax.experimental import pallas as pl
from jax.experimental.pallas import tpu as pltpu
from jax.sharding import PartitionSpec as P

VARS = 5
RHS = 8
REACH = 3
SLOTS = 2
STATE = REACH * VARS
LANES = 128
PAIR = VARS * VARS * SLOTS
FWIDE = 24
GWIDE = 16
SLOT = 8
FULL, MAP, ONE = 3, 2, 1
F32 = jnp.float32
VMEM = pltpu.VMEM
MESH = pl.DeviceIdType.MESH
VMEM_LIMIT = 61 << 20
UNROLL = 4


def row(ref, *index):
    *lead, at = index
    return ref[(*lead, pl.ds(at, RHS, stride=0), slice(None))]


def lanes_of(shape):
    return lax.broadcasted_iota(jnp.int32, shape, len(shape) - 1)


def chunk(t):
    return slice(8 * t, 8 * t + 8)


def near(cols, counts, side, slot, b, start, forward, absent):
    col = cols[slot, b] - start
    used = slot < counts[side, b]
    return jnp.where(used, col + REACH if forward else col, absent)


def couple(coef, dinv, out, blocks):
    for group in range(blocks // 8):
        rows = pl.ds(8 * group, 8)
        inv = [dinv[q, rows, :] for q in range(VARS * VARS)]
        for slot in range(SLOTS):
            for j in range(VARS):
                col = [
                    coef[pl.ds(8 * group * PAIR + (m * VARS + j) * SLOTS + slot, 8, stride=PAIR), :]
                    for m in range(VARS)
                ]
                for i in range(VARS):
                    acc = inv[i * VARS] * col[0]
                    for m in range(1, VARS):
                        acc = acc + inv[i * VARS + m] * col[m]
                    out[slot * 25 + i * VARS + j, rows, :] = acc


def coupled(coef, b, values, emit):
    for i in range(VARS):
        part = []
        for k in range(SLOTS):
            acc = None
            for j in range(VARS):
                c = row(coef, k * 25 + i * VARS + j, b)
                new = [c * x for x in values[k][j]]
                acc = new if acc is None else [p + q for p, q in zip(acc, new)]
            part.append(acc)
        for t, (p, q) in enumerate(zip(*part)):
            emit(i, t, p + q)


def pack(vals, tiles, send):
    half = LANES // 2
    for tile in range(tiles):
        turned = vals[tile * LANES : (tile + 1) * LANES, :].T
        for c in range(2):
            for first in range(0, half, 8):
                at = first * SLOT + c * tiles + tile
                send[pl.ds(at, 8, stride=SLOT), :] = turned[c * half + first : c * half + first + 8]


def unpack(recv, tiles, vals):
    half = LANES // 2
    for tile in range(tiles):
        both = [recv[pl.ds(c * tiles + tile, half, stride=SLOT), :] for c in range(2)]
        vals[tile * LANES : (tile + 1) * LANES, :] = jnp.concatenate(both, 0).T


def shifts(span):
    return [1 << n for n in range(span.bit_length() - 1)]


def turned(x, shift, ahead):
    return pltpu.roll(x, LANES - shift if ahead else shift, 1)


def scan_maps(stack, lane, span, ahead):
    for n, shift in enumerate(shifts(span)[:-1]):
        inside = lane < span - shift if ahead else lane >= shift
        for t in range(2):
            e = [turned(stack[n, j, chunk(t), :], shift, ahead) for j in range(STATE)]
            for i in range(STATE):
                acc = None
                for j in range(STATE):
                    term = row(stack, n, i, j) * e[j]
                    acc = term if acc is None else acc + term
                stack[n + 1, i, chunk(t), :] = jnp.where(inside, acc, stack[n, i, chunk(t), :])


def scan_states(stack, state, lane, span, ahead):
    for n, shift in enumerate(shifts(span)):
        inside = lane < span - shift if ahead else lane >= shift
        e = [turned(x, shift, ahead) for x in state]
        fresh = []
        for i in range(STATE):
            acc = state[i]
            for j in range(STATE):
                acc = acc + row(stack, n, i, j) * e[j]
            fresh.append(jnp.where(inside, acc, state[i]))
        state = fresh
    edge = lane == span - 1 if ahead else lane == 0
    return [jnp.where(edge, 0.0, turned(x, 1, ahead)) for x in state]


def main_kernel(
    nodes, subs, line, lcol_in, ucol_in, counts_in, rhs_in, dinv_in, low_in, up_in, side_in,
    corr_out, resid_out, total,
    lcol, ucol, counts, resid, sided, rhs, dinv, low, up, side, alow, aup, y, zb, zm, vals,
    s1, s2, s3, r1, r2, r3, s4, s5, r4, r5, gf, gb,
    zpad, upad, before, outer, edges, beside, part, stage, wide, deep,
    load_sem, send_sem, recv_sem, own_sem, out_sem,
):
    blocks = rhs.shape[0]
    me, sub = lax.axis_index("chain"), lax.axis_index("sub")
    start, absent = me * blocks, blocks + REACH
    loads = [
        pltpu.make_async_copy(src, dst, load_sem.at[n])
        for n, (src, dst) in enumerate(
            (
                (low_in, low), (dinv_in, dinv), (rhs_in, rhs), (up_in, up), (side_in, side),
                (lcol_in, lcol), (ucol_in, ucol), (counts_in, counts),
            )
        )
    ]
    for load in loads:
        load.start()

    barrier = pltpu.get_barrier_semaphore()
    flat = (me // line) * subs + sub
    place = lax.rem(me, line)

    def cross(k):
        other = lax.rem(flat + k, subs * (nodes // line))
        return {"chain": (other // subs) * line + place, "sub": lax.rem(other, subs)}

    def along(k):
        return {"chain": me - place + lax.rem(place + k, line)}

    def around(k):
        return {"chain": lax.rem(me + k, nodes)}

    across = subs * (nodes // line)
    spans = ((nodes // 2, nodes), (nodes // 4, nodes // 2), (1, nodes // 4))
    for peer, spans_of in ((around, spans[:1]), (cross, ((1, across),)), (around, spans[1:])):
        for low_k, high_k in spans_of:

            def greet(k, carry, peer=peer):
                pl.semaphore_signal(barrier, inc=1, device_id=peer(k), device_id_type=MESH)
                return carry

            lax.fori_loop(low_k, high_k, greet, 0)

    def remote(src, dst, n, peer):
        return pltpu.make_async_remote_copy(
            src_ref=src,
            dst_ref=dst,
            send_sem=send_sem.at[n],
            recv_sem=recv_sem.at[n],
            device_id=peer,
            device_id_type=MESH,
        )

    mine = pl.multiple_of(me * SLOT, SLOT)

    def own(src, dst, tiles, n):
        rows = pl.ds(mine, 2 * tiles)
        return pltpu.make_async_copy(src.at[rows], dst.at[rows], own_sem.at[n])

    def post(src, dst, tiles, n):
        own(src, dst, tiles, n).start()

        def one(k, carry):
            to = lax.rem(me + k, nodes)
            there = pl.ds(pl.multiple_of(to * SLOT, SLOT), 2 * tiles)
            remote(src.at[there], dst.at[pl.ds(mine, 2 * tiles)], n, {"chain": to}).start()
            return carry

        for low_k, high_k in spans:
            lax.fori_loop(low_k, high_k, one, 0)

    def whole(src, dst, tiles, n):
        rows = pl.ds(0, 2 * tiles * (nodes - 1))
        return remote(src.at[rows], dst.at[rows], n, around(1))

    def collect(src, dst, tiles, n):
        own(src, dst, tiles, n).wait()
        whole(src, dst, tiles, n).wait_recv()

    fsub = lax.broadcasted_iota(jnp.int32, (FWIDE, LANES), 0)
    gsub = lax.broadcasted_iota(jnp.int32, (GWIDE, LANES), 0)
    for d in range(1, REACH + 1):
        for v in range(VARS):
            q = (d - 1) * VARS + v
            y[REACH - d, v] = jnp.where(fsub == RHS + q, 1.0, 0.0).astype(F32)
            zb[blocks - 1 + d, v] = jnp.where(gsub == q, 1.0, 0.0).astype(F32)
            zm[blocks - 1 + d, v] = jnp.zeros((FWIDE, LANES), F32)
    none = jnp.zeros((RHS, LANES), F32)
    for v in range(VARS):
        y[absent, v] = jnp.zeros((FWIDE, LANES), F32)
        zm[absent, v] = jnp.zeros((FWIDE, LANES), F32)
        zb[absent, v] = jnp.zeros((GWIDE, LANES), F32)
        zpad[absent, v] = none
        upad[absent, v] = none
    vals[...] = jnp.zeros(vals.shape, F32)

    def lower(b):
        return [near(lcol, counts, 0, k, b, start, True, absent) for k in range(SLOTS)]

    def upper(b):
        return [near(ucol, counts, 1, k, b, start, False, absent) for k in range(SLOTS)]

    def window(ref, at, chunks):
        return [
            [[ref[at[k], j, chunk(t), :] for t in range(chunks)] for j in range(VARS)]
            for k in range(SLOTS)
        ]

    for n in (5, 6, 7, 0, 1):
        loads[n].wait()
    couple(low, dinv, alow, blocks)
    loads[2].wait()

    def forward(b, carry):
        values = window(y, lower(b), 3)
        src = [rhs[b, m] for m in range(VARS)]
        own_part = []
        for i in range(VARS):
            w = row(dinv, i * VARS, b) * src[0]
            for m in range(1, VARS):
                w = w + row(dinv, i * VARS + m, b) * src[m]
            own_part.append(w)

        def emit(i, t, value):
            y[b + REACH, i, chunk(t), :] = own_part[i] - value if t == 0 else -value

        coupled(alow, b, values, emit)
        return carry

    lax.fori_loop(0, blocks, forward, 0)
    for d in range(1, REACH + 1):
        for v in range(VARS):
            q = (d - 1) * VARS + v
            vals[q * FWIDE : (q + 1) * FWIDE, :] = y[REACH + blocks - d, v]
    pack(vals, FULL, s1)
    loads[3].wait()
    couple(up, dinv, aup, blocks)

    def basis(step, carry):
        b = blocks - 1 - step

        def emit(i, t, value):
            zb[b, i, chunk(t), :] = -value

        coupled(aup, b, window(zb, upper(b), 2), emit)
        return carry

    lax.fori_loop(0, blocks, basis, 0)
    for d in range(1, REACH + 1):
        for v in range(VARS):
            q = (d - 1) * VARS + v
            vals[q * GWIDE : (q + 1) * GWIDE, :] = zb[d - 1, v]
    pack(vals, MAP, s2)
    def backward(step, carry):
        b = blocks - 1 - step

        def emit(i, t, value):
            zm[b, i, chunk(t), :] = y[b + REACH, i, chunk(t), :] - value

        coupled(aup, b, window(zm, upper(b), 3), emit)
        return carry

    lax.fori_loop(0, blocks, backward, 0)
    for d in range(1, REACH + 1):
        for v in range(VARS):
            q = (d - 1) * VARS + v
            vals[q * FWIDE : (q + 1) * FWIDE, :] = zm[d - 1, v]
    pack(vals, FULL, s3)
    pl.semaphore_wait(barrier, nodes + across - 2)
    post(s1, r1, FULL, 0)
    post(s2, r2, MAP, 1)
    post(s3, r3, FULL, 2)

    lane = lanes_of((RHS, LANES))
    at = lax.rem(lane, nodes)
    collect(s1, r1, FULL, 0)
    unpack(r1, FULL, vals)
    for i in range(STATE):
        gf[0, i] = vals[i * FWIDE + RHS : (i + 1) * FWIDE, :]
    scan_maps(gf, at, nodes, False)
    entering = scan_states(
        gf, [vals[i * FWIDE : i * FWIDE + RHS, :] for i in range(STATE)], at, nodes, False
    )
    vals[STATE * RHS : LANES, :] = none
    for i in range(STATE):
        vals[i * RHS : (i + 1) * RHS, :] = entering[i]
    pack(vals, ONE, s4)
    post(s4, r4, ONE, 3)

    collect(s2, r2, MAP, 1)
    unpack(r2, MAP, vals)
    for i in range(STATE):
        gb[0, i] = vals[i * GWIDE : (i + 1) * GWIDE, :]
    scan_maps(gb, at, nodes, True)
    collect(s3, r3, FULL, 2)
    unpack(r3, FULL, vals)
    state = []
    for i in range(STATE):
        acc = vals[i * FWIDE : i * FWIDE + RHS, :]
        for j in range(STATE):
            acc = acc + row(vals, i * FWIDE + RHS + j) * entering[j]
        state.append(acc)
    following = scan_states(gb, state, at, nodes, True)
    vals[STATE * RHS : LANES, :] = none
    for i in range(STATE):
        vals[i * RHS : (i + 1) * RHS, :] = following[i]
    pack(vals, ONE, s5)
    post(s5, r5, ONE, 4)

    collect(s4, r4, ONE, 3)
    unpack(r4, ONE, vals)
    entering = [vals[i * RHS : (i + 1) * RHS, :] for i in range(STATE)]

    def enter(b, carry):
        for i in range(VARS):
            acc = zm[b, i, chunk(0), :]
            for j in range(STATE):
                acc = acc + row(zm, b, i, RHS + j) * entering[j]
            zpad[b, i] = acc
        return carry

    lax.fori_loop(0, blocks, enter, 0)
    collect(s5, r5, ONE, 4)
    unpack(r5, ONE, vals)
    following = [vals[i * RHS : (i + 1) * RHS, :] for i in range(STATE)]
    for d in range(1, REACH + 1):
        for v in range(VARS):
            zpad[blocks - 1 + d, v] = following[(d - 1) * VARS + v]

    def follow(b, carry):
        for i in range(VARS):
            acc = zpad[b, i]
            for j in range(STATE):
                acc = acc + row(zb, b, i, j) * following[j]
            zpad[b, i] = acc
        return carry

    lax.fori_loop(0, blocks, follow, 0)
    rows_of = zpad.reshape(zpad.shape[0] * VARS * RHS, LANES)
    for tile in range(RHS):
        columns = rows_of[tile * LANES : (tile + 1) * LANES, :].T
        edges[0, tile : tile + 1, :] = columns[0:1]
        edges[1, tile : tile + 1, :] = columns[LANES - 1 :]
    left, right = lax.rem(sub + subs - 1, subs), lax.rem(sub + 1, subs)
    halo = [
        remote(edges.at[1], beside.at[0], 5, {"sub": right}),
        remote(edges.at[0], beside.at[1], 6, {"sub": left}),
        remote(upad.at[pl.ds(blocks, REACH)], before, 7, around(1)),
    ]
    halo[0].start()
    halo[1].start()
    store_corr = pltpu.make_async_copy(zpad.at[pl.ds(0, blocks)], corr_out, out_sem.at[0])
    store_corr.start()

    def difference(step, carry):
        b = blocks - 1 - step

        def emit(i, t, value):
            upad[b + REACH, i] = value

        at = upper(b)
        values = [[[zpad[at[k], j]] for j in range(VARS)] for k in range(SLOTS)]
        coupled(aup, b, values, emit)
        return carry

    lax.fori_loop(0, REACH, difference, 0)
    halo[2].start()
    lax.fori_loop(REACH, blocks, difference, 0)

    def apply(coef, b, i, values):
        total = None
        for k, column in enumerate(values):
            acc = None
            for j in range(VARS):
                term = row(coef, b * PAIR + (i * VARS + j) * SLOTS + k) * column[j]
                acc = term if acc is None else acc + term
            total = acc if total is None else total + acc
        return total

    def before_part(b, carry):
        at = lower(b)
        values = [[upad[at[k], j] for j in range(VARS)] for k in range(SLOTS)]
        for i in range(VARS):
            resid[b, i] = apply(low, b, i, values)
        return carry

    lax.fori_loop(REACH, blocks, before_part, 0)
    loads[4].wait()

    def inner_part(b, carry):
        west, east = [], []
        for j in range(VARS):
            value = zpad[b, j]
            west.append(jnp.where(lane == 0, 0.0, pltpu.roll(value, 1, 1)))
            east.append(jnp.where(lane == LANES - 1, 0.0, pltpu.roll(value, LANES - 1, 1)))
        for i in range(VARS):
            sided[b, i] = apply(side, b, i, (west, east))
        return carry

    def inner_parts(n, carry):
        for m in range(UNROLL):
            inner_part(n * UNROLL + m, carry)
        return carry

    lax.fori_loop(0, blocks // UNROLL, inner_parts, 0)
    halo[2].wait_recv()
    for d in range(REACH):
        for v in range(VARS):
            upad[d, v] = jnp.where(me == 0, 0.0, before[d, v])
    lax.fori_loop(0, REACH, before_part, 0)
    halo[0].wait_recv()
    halo[1].wait_recv()
    whole_row = (LANES, LANES)
    index = lax.broadcasted_iota(jnp.int32, whole_row, 0)
    for tile in range(RHS):
        west = jnp.where(sub == 0, 0.0, beside[0, tile : tile + 1, :])
        east = jnp.where(sub == subs - 1, 0.0, beside[1, tile : tile + 1, :])
        rows = jnp.where(
            index == 0,
            jnp.broadcast_to(west, whole_row),
            jnp.where(index == LANES - 1, jnp.broadcast_to(east, whole_row), 0.0),
        )
        outer[tile * LANES : (tile + 1) * LANES, :] = rows.T

    def edge_part(b, square):
        edge = [
            outer[pl.ds(pl.multiple_of((b * VARS + j) * RHS, RHS), RHS), :] for j in range(VARS)
        ]
        for i in range(VARS):
            value = resid[b, i] - sided[b, i]
            acc = None
            for j in range(VARS):
                at = b * PAIR + (i * VARS + j) * SLOTS
                term = jnp.where(lane == 0, row(side, at), row(side, at + 1)) * edge[j]
                acc = term if acc is None else acc + term
            value = value - acc
            resid[b, i] = value
            square = square + value * value
        return square

    def edge_parts(n, square):
        for m in range(UNROLL):
            square = edge_part(n * UNROLL + m, square)
        return square

    square = lax.fori_loop(0, blocks // UNROLL, edge_parts, none)
    store_resid = pltpu.make_async_copy(resid, resid_out, out_sem.at[1])
    store_resid.start()
    sums = jnp.sum(square, axis=1, keepdims=True)
    diagonal = lax.broadcasted_iota(jnp.int32, (RHS, LANES), 0) == lane
    part[...] = jnp.sum(jnp.where(diagonal, sums, 0.0), axis=0, keepdims=True)

    rounds = ((along, line, place, part, wide, stage), (cross, across, flat, stage, deep, total))
    for n, (peer, count, index, src, dst, out) in enumerate(rounds):

        def tell(k, carry, peer=peer, src=src, dst=dst, index=index, n=n):
            remote(src, dst.at[index], 8 + n, peer(k)).start()
            return carry

        lax.fori_loop(1, count, tell, 0)
        mine_too = pltpu.make_async_copy(src, dst.at[index], own_sem.at[5 + n])
        mine_too.start()
        mine_too.wait()
        rows = pl.ds(0, count - 1)
        remote(dst.at[rows], dst.at[rows], 8 + n, peer(1)).wait_recv()
        out[...] = jnp.sum(dst[...], axis=0)

    store_corr.wait()
    store_resid.wait()
    for src, dst, tiles, n in (
        (s1, r1, FULL, 0), (s2, r2, MAP, 1), (s3, r3, FULL, 2), (s4, r4, ONE, 3), (s5, r5, ONE, 4)
    ):
        whole(src, dst, tiles, n).wait_send()
    for copy in halo:
        copy.wait_send()
    for n, (peer, count, _, _, dst, _) in enumerate(rounds):
        rows = pl.ds(0, count - 1)
        remote(dst.at[rows], dst.at[rows], 8 + n, peer(1)).wait_send()


def scale_kernel(entries, corr, resid, total, corr_out, out, held, piece, sums_in, load_sem, store_sem):
    parts = piece.shape[0] // 8
    rows = [pl.ds(8 * n, 8) for n in range(parts)]
    loads = [pltpu.make_async_copy(total, sums_in, load_sem.at[parts])]
    loads += [pltpu.make_async_copy(resid.at[r], piece.at[r], load_sem.at[n]) for n, r in enumerate(rows)]
    loads += [pltpu.make_async_copy(corr, held, load_sem.at[parts + 1])]
    stores = [pltpu.make_async_copy(piece.at[r], out.at[r], store_sem.at[n]) for n, r in enumerate(rows)]
    stores += [pltpu.make_async_copy(held, corr_out, store_sem.at[parts])]
    for load in loads:
        load.start()
    lane = lanes_of((RHS, LANES))
    diagonal = lax.broadcasted_iota(jnp.int32, (RHS, LANES), 0) == lane
    loads[0].wait()
    wide = jnp.broadcast_to(sums_in[...], (RHS, LANES))
    sums = jnp.sum(jnp.where(diagonal, wide, 0.0), axis=1, keepdims=True)
    factor = jnp.broadcast_to(lax.rsqrt(sums / entries + 1e-6), (RHS, LANES))
    for n, r in enumerate(rows):
        loads[1 + n].wait()
        piece[r] = piece[r] * factor[None, None]
        stores[n].start()
    loads[-1].wait()
    stores[-1].start()
    for store in stores:
        store.wait()


def spec(space):
    return pl.BlockSpec(memory_space=space)


def shards(nodes, subs, line, rhs, diag_block, diag_inverse, lower_coef, upper_coef, side_coef, lower_cols, upper_cols, counts):
    blocks = rhs.shape[0]
    cells = rhs.shape[3]
    padded = blocks + REACH + 1
    across = subs * (nodes // line)
    dinv = jnp.transpose(diag_inverse, (1, 2, 0, 3)).reshape(VARS * VARS, blocks, cells)
    low, up, side = (
        jnp.transpose(x, (0, 2, 3, 1, 4)).reshape(blocks * PAIR, cells)
        for x in (lower_coef, upper_coef, side_coef)
    )
    plane = jax.ShapeDtypeStruct((blocks, VARS, RHS, cells), F32)
    slots = VMEM((nodes * SLOT, cells), F32)
    window = VMEM((padded, VARS, RHS, cells), F32)
    depth = len(shifts(nodes))
    corr, resid, total = pl.pallas_call(
        functools.partial(main_kernel, nodes, subs, line),
        out_shape=(plane, plane, jax.ShapeDtypeStruct((1, cells), F32)),
        in_specs=[spec(pl.ANY)] * 8,
        out_specs=(spec(pl.ANY), spec(pl.ANY), spec(VMEM)),
        scratch_shapes=[pltpu.SMEM((SLOTS, blocks), jnp.int32)] * 3
        + [VMEM(plane.shape, F32)] * 2
        + [VMEM(x.shape, F32) for x in (rhs, dinv, low, up, side)]
        + [VMEM((PAIR, blocks, cells), F32)] * 2
        + [VMEM((padded, VARS, wide, cells), F32) for wide in (FWIDE, GWIDE, FWIDE)]
        + [VMEM((FULL * LANES, cells), F32)]
        + [slots] * 10
        + [VMEM((depth, STATE, GWIDE, cells), F32)] * 2
        + [window] * 2
        + [VMEM((REACH, VARS, RHS, cells), F32)]
        + [VMEM((RHS * LANES, cells), F32)]
        + [VMEM((2, RHS, cells), F32)] * 2
        + [VMEM((1, cells), F32)] * 2
        + [VMEM((line, 1, cells), F32), VMEM((across, 1, cells), F32)]
        + [pltpu.SemaphoreType.DMA((n,)) for n in (8, 10, 10, 7, 2)],
        compiler_params=pltpu.CompilerParams(
            collective_id=0, has_side_effects=True, vmem_limit_bytes=VMEM_LIMIT
        ),
        name="sweeps",
    )(lower_cols.T, upper_cols.T, counts.T, rhs, dinv, low, up, side)
    entries = nodes * blocks * VARS * subs * cells
    return pl.pallas_call(
        functools.partial(scale_kernel, entries),
        out_shape=(plane, plane),
        in_specs=[spec(pl.ANY)] * 3,
        out_specs=(spec(pl.ANY),) * 2,
        scratch_shapes=[VMEM(plane.shape, F32)] * 2
        + [VMEM((1, cells), F32)]
        + [pltpu.SemaphoreType.DMA((blocks // 8 + n,)) for n in (2, 1)],
        compiler_params=pltpu.CompilerParams(vmem_limit_bytes=VMEM_LIMIT),
        name="scale",
    )(corr, resid, total)


def solution(mesh):
    nodes, subs = mesh.shape["chain"], mesh.shape["sub"]
    line = 16 if nodes % 16 == 0 else nodes
    plane = P("chain", None, None, "sub")
    coef = P("chain", None, None, None, "sub")
    return jax.shard_map(
        functools.partial(shards, nodes, subs, line),
        mesh=mesh,
        in_specs=(plane, plane, plane, coef, coef, coef, P("chain", None), P("chain", None), P("chain", None)),
        out_specs=(plane, plane),
        check_vma=False,
    )
```

```python
import functools

import jax
import jax.numpy as jnp
from jax import lax
from jax.experimental import pallas as pl
from jax.experimental.pallas import tpu as pltpu
from jax.sharding import PartitionSpec as P

VARS = 5
RHS = 8
REACH = 3
SLOTS = 2
STATE = REACH * VARS
LANES = 128
PAIR = VARS * VARS * SLOTS
FWIDE = 24
GWIDE = 16
SLOT = 8
FULL, MAP, ONE = 3, 2, 1
F32 = jnp.float32
VMEM = pltpu.VMEM
MESH = pl.DeviceIdType.MESH
VMEM_LIMIT = 61 << 20
UNROLL = 4


def row(ref, *index):
    *lead, at = index
    return ref[(*lead, pl.ds(at, RHS, stride=0), slice(None))]


def lanes_of(shape):
    return lax.broadcasted_iota(jnp.int32, shape, len(shape) - 1)


def chunk(t):
    return slice(8 * t, 8 * t + 8)


def near(cols, counts, side, slot, b, start, forward, absent):
    col = cols[slot, b] - start
    used = slot < counts[side, b]
    return jnp.where(used, col + REACH if forward else col, absent)


def couple(coef, dinv, out, blocks):
    for group in range(blocks // 8):
        rows = pl.ds(8 * group, 8)
        inv = [dinv[q, rows, :] for q in range(VARS * VARS)]
        for slot in range(SLOTS):
            for j in range(VARS):
                col = [
                    coef[pl.ds(8 * group * PAIR + (m * VARS + j) * SLOTS + slot, 8, stride=PAIR), :]
                    for m in range(VARS)
                ]
                for i in range(VARS):
                    acc = inv[i * VARS] * col[0]
                    for m in range(1, VARS):
                        acc = acc + inv[i * VARS + m] * col[m]
                    out[slot * 25 + i * VARS + j, rows, :] = acc


def coupled(coef, b, values, emit):
    for i in range(VARS):
        part = []
        for k in range(SLOTS):
            acc = None
            for j in range(VARS):
                c = row(coef, k * 25 + i * VARS + j, b)
                new = [c * x for x in values[k][j]]
                acc = new if acc is None else [p + q for p, q in zip(acc, new)]
            part.append(acc)
        for t, (p, q) in enumerate(zip(*part)):
            emit(i, t, p + q)


def pack(vals, tiles, send, span):
    for tile in range(tiles):
        turned = vals[tile * LANES : (tile + 1) * LANES, :].T
        for c in range(2):
            for first in range(0, span, 8):
                at = first * SLOT + c * tiles + tile
                send[pl.ds(at, 8, stride=SLOT), :] = turned[c * span + first : c * span + first + 8]


def unpack(recv, tiles, vals, span):
    for tile in range(tiles):
        both = [recv[pl.ds(c * tiles + tile, span, stride=SLOT), :] for c in range(2)]
        both = both * (LANES // (2 * span))
        vals[tile * LANES : (tile + 1) * LANES, :] = jnp.concatenate(both, 0).T


def times(coef, values, start):
    out = []
    for i in range(STATE):
        acc = list(start(i))
        for j in range(STATE):
            c = coef(i, j)
            acc = [c * x if a is None else a + c * x for a, x in zip(acc, values[j])]
        out.append(acc)
    return out


def shifts(span):
    return [1 << n for n in range(span.bit_length() - 1)]


def turned(x, shift, ahead):
    return pltpu.roll(x, LANES - shift if ahead else shift, 1)


def scan_maps(stack, lane, span, ahead):
    for n, shift in enumerate(shifts(span)[:-1]):
        inside = lane < span - shift if ahead else lane >= shift
        for t in range(2):
            e = [turned(stack[n, j, chunk(t), :], shift, ahead) for j in range(STATE)]
            for i in range(STATE):
                acc = None
                for j in range(STATE):
                    term = row(stack, n, i, j) * e[j]
                    acc = term if acc is None else acc + term
                stack[n + 1, i, chunk(t), :] = jnp.where(inside, acc, stack[n, i, chunk(t), :])


def scan_states(stack, state, lane, span, ahead):
    for n, shift in enumerate(shifts(span)):
        inside = lane < span - shift if ahead else lane >= shift
        e = [turned(x, shift, ahead) for x in state]
        fresh = []
        for i in range(STATE):
            acc = state[i]
            for j in range(STATE):
                acc = acc + row(stack, n, i, j) * e[j]
            fresh.append(jnp.where(inside, acc, state[i]))
        state = fresh
    edge = lane == span - 1 if ahead else lane == 0
    return [jnp.where(edge, 0.0, turned(x, 1, ahead)) for x in state]


def main_kernel(
    nodes, subs, line, lcol_in, ucol_in, counts_in, rhs_in, dinv_in, low_in, up_in, side_in,
    corr_out, resid_out, total,
    lcol, ucol, counts, resid, sided, rhs, dinv, low, up, side, alow, aup, y, zb, zm, vals,
    s1, s2, s3, r4, r5, r1, r2, r3, s4, s5, gf, gb, yp, zbp, zmp, mid, enters, follows,
    zpad, upad, before, outer, edges, beside, part, stage, wide, deep,
    load_sem, send_sem, recv_sem, own_sem, out_sem,
):
    blocks = rhs.shape[0]
    me, sub = lax.axis_index("chain"), lax.axis_index("sub")
    start, absent = me * blocks, blocks + REACH
    loads = [
        pltpu.make_async_copy(src, dst, load_sem.at[n])
        for n, (src, dst) in enumerate(
            (
                (low_in, low), (dinv_in, dinv), (rhs_in, rhs), (up_in, up), (side_in, side),
                (lcol_in, lcol), (ucol_in, ucol), (counts_in, counts),
            )
        )
    ]
    for load in loads:
        load.start()

    barrier = pltpu.get_barrier_semaphore()
    flat = (me // line) * subs + sub
    place = lax.rem(me, line)

    def cross(k):
        other = lax.rem(flat + k, subs * (nodes // line))
        return {"chain": (other // subs) * line + place, "sub": lax.rem(other, subs)}

    def along(k):
        return {"chain": me - place + lax.rem(place + k, line)}

    def around(k):
        return {"chain": lax.rem(me + k, nodes)}

    across = subs * (nodes // line)
    spans = ((nodes // 2, nodes), (nodes // 4, nodes // 2), (1, nodes // 4))
    for peer, spans_of in ((around, spans[:1]), (cross, ((1, across),)), (around, spans[1:])):
        for low_k, high_k in spans_of:

            def greet(k, carry, peer=peer):
                pl.semaphore_signal(barrier, inc=1, device_id=peer(k), device_id_type=MESH)
                return carry

            lax.fori_loop(low_k, high_k, greet, 0)

    def remote(src, dst, n, peer):
        return pltpu.make_async_remote_copy(
            src_ref=src,
            dst_ref=dst,
            send_sem=send_sem.at[n],
            recv_sem=recv_sem.at[n],
            device_id=peer,
            device_id_type=MESH,
        )

    chips, chip, core = nodes // 2, me // 2, lax.rem(me, 2)

    def slot(n, tiles):
        return pl.ds(pl.multiple_of(n * SLOT, SLOT), 2 * tiles)

    def own(src, dst, tiles, n, out, inside):
        return pltpu.make_async_copy(src.at[slot(out, tiles)], dst.at[slot(inside, tiles)], own_sem.at[n])

    def post(src, dst, tiles, n, out, inside):
        own(src, dst, tiles, n, out(me), inside).start()

        def one(k, carry):
            to = lax.rem(me + k, nodes)
            remote(src.at[slot(out(to), tiles)], dst.at[slot(inside, tiles)], n, {"chain": to}).start()
            return carry

        for low_k, high_k in spans:
            lax.fori_loop(low_k, high_k, one, 0)

    def whole(ref, tiles, n, count):
        rows = pl.ds(0, 2 * tiles * count)
        return remote(ref.at[rows], ref.at[rows], n, around(1))

    def post_map(src, dst, tiles, n):
        post(src, dst, tiles, n, lambda to: to, chip)

    def post_state(src, dst, n):
        post(src, dst, ONE, n, lambda to: to // 2, me)

    def collect_map(src, dst, tiles, n, sender):
        @pl.when(core == sender)
        def _():
            own(src, dst, tiles, n, me, chip).wait()
            whole(dst, tiles, n, chips - 1).wait_recv()

        @pl.when(core != sender)
        def _():
            whole(dst, tiles, n, chips).wait_recv()

    def collect_state(src, dst, n):
        own(src, dst, ONE, n, chip, me).wait()
        whole(dst, ONE, n, nodes - 1).wait_recv()

    fsub = lax.broadcasted_iota(jnp.int32, (FWIDE, LANES), 0)
    gsub = lax.broadcasted_iota(jnp.int32, (GWIDE, LANES), 0)
    for d in range(1, REACH + 1):
        for v in range(VARS):
            q = (d - 1) * VARS + v
            y[REACH - d, v] = jnp.where(fsub == RHS + q, 1.0, 0.0).astype(F32)
            zb[blocks - 1 + d, v] = jnp.where(gsub == q, 1.0, 0.0).astype(F32)
            zm[blocks - 1 + d, v] = jnp.zeros((FWIDE, LANES), F32)
    none = jnp.zeros((RHS, LANES), F32)
    for v in range(VARS):
        y[absent, v] = jnp.zeros((FWIDE, LANES), F32)
        zm[absent, v] = jnp.zeros((FWIDE, LANES), F32)
        zb[absent, v] = jnp.zeros((GWIDE, LANES), F32)
        zpad[absent, v] = none
        upad[absent, v] = none
    vals[...] = jnp.zeros(vals.shape, F32)

    def lower(b):
        return [near(lcol, counts, 0, k, b, start, True, absent) for k in range(SLOTS)]

    def upper(b):
        return [near(ucol, counts, 1, k, b, start, False, absent) for k in range(SLOTS)]

    def window(ref, at, chunks):
        return [
            [[ref[at[k], j, chunk(t), :] for t in range(chunks)] for j in range(VARS)]
            for k in range(SLOTS)
        ]

    for n in (5, 6, 7, 0, 1):
        loads[n].wait()
    couple(low, dinv, alow, blocks)
    loads[2].wait()

    def forward(b, carry):
        values = window(y, lower(b), 3)
        src = [rhs[b, m] for m in range(VARS)]
        own_part = []
        for i in range(VARS):
            w = row(dinv, i * VARS, b) * src[0]
            for m in range(1, VARS):
                w = w + row(dinv, i * VARS + m, b) * src[m]
            own_part.append(w)

        def emit(i, t, value):
            y[b + REACH, i, chunk(t), :] = own_part[i] - value if t == 0 else -value

        coupled(alow, b, values, emit)
        return carry

    lax.fori_loop(0, blocks, forward, 0)

    loads[3].wait()
    couple(up, dinv, aup, blocks)

    def basis(step, carry):
        b = blocks - 1 - step

        def emit(i, t, value):
            zb[b, i, chunk(t), :] = -value

        coupled(aup, b, window(zb, upper(b), 2), emit)
        return carry

    lax.fori_loop(0, blocks, basis, 0)

    def backward(step, carry):
        b = blocks - 1 - step

        def emit(i, t, value):
            zm[b, i, chunk(t), :] = y[b + REACH, i, chunk(t), :] - value

        coupled(aup, b, window(zm, upper(b), 3), emit)
        return carry

    lax.fori_loop(0, blocks, backward, 0)
    pl.semaphore_wait(barrier, nodes + across - 2)

    partner = {"chain": me + 1 - 2 * core}
    ends = (y.at[pl.ds(blocks, REACH)], zb.at[pl.ds(0, REACH)], zm.at[pl.ds(0, REACH)])
    pairs = [
        remote(src, dst, 10 + n, partner) for n, (src, dst) in enumerate(zip(ends, (yp, zbp, zmp)))
    ]
    for copy in pairs:
        copy.start()

    def at_state(q):
        return q // VARS, q % VARS

    def forward_at(ref, last):
        def index(q):
            d, v = at_state(q)
            return ref, last - d, v

        return index

    def backward_at(ref):
        def index(q):
            d, v = at_state(q)
            return ref, d, v

        return index

    def chunks(index, span):
        parts = []
        for q in range(STATE):
            ref, d, v = index(q)
            parts.append([ref[d, v, chunk(t), :] for t in span])
        return parts

    def entry(index, offset):
        def coef(i, j):
            ref, d, v = index(i)
            return row(ref, d, v, offset + j)

        return coef

    mine_f, mine_b, mine_m = forward_at(y, blocks + REACH - 1), backward_at(zb), backward_at(zm)
    other_f, other_b, other_m = forward_at(yp, REACH - 1), backward_at(zbp), backward_at(zmp)

    def put(out, wide, parts):
        for i, part in enumerate(parts):
            for t, value in enumerate(part):
                out[i * wide + 8 * t : i * wide + 8 * t + 8, :] = value

    pairs[0].wait_recv()

    @pl.when(core == 0)
    def _():
        heads = chunks(other_f, (0,))
        for t in range(3):
            values = chunks(mine_f, (t,))
            start_of = (lambda i: heads[i]) if t == 0 else (lambda i: [None])
            for i, (value,) in enumerate(times(entry(other_f, RHS), values, start_of)):
                vals[i * FWIDE + 8 * t : i * FWIDE + 8 * t + 8, :] = value
        pack(vals, FULL, s1, nodes)
        post_map(s1, r1, FULL, 0)
        pairs[1].wait_recv()
        values = chunks(other_b, (0, 1))
        put(vals, GWIDE, times(entry(mine_b, 0), values, lambda i: [None, None]))
        pack(vals, MAP, s2, nodes)
        post_map(s2, r2, MAP, 1)
        pairs[2].wait_recv()

    @pl.when(core == 1)
    def _():
        heads = chunks(mine_m, (0,))
        for t in range(3):
            values = chunks(other_f, (t,))
            start_of = (lambda i: heads[i]) if t == 0 else (lambda i: [None])
            for i, (value,) in enumerate(times(entry(mine_m, RHS), values, start_of)):
                mid[i, chunk(t), :] = value
        pairs[1].wait_recv()
        pairs[2].wait_recv()
        for t in range(3):
            values = [[mid[j, chunk(t), :]] for j in range(STATE)]
            heads = chunks(other_m, (t,))
            for i, (value,) in enumerate(times(entry(other_b, 0), values, lambda i: heads[i])):
                vals[i * FWIDE + 8 * t : i * FWIDE + 8 * t + 8, :] = value
        pack(vals, FULL, s3, nodes)
        post_map(s3, r3, FULL, 2)

    lane = lanes_of((RHS, LANES))
    at = lax.rem(lane, chips)
    collect_map(s1, r1, FULL, 0, 0)
    unpack(r1, FULL, vals, chips)
    for i in range(STATE):
        gf[0, i] = vals[i * FWIDE + RHS : (i + 1) * FWIDE, :]
    scan_maps(gf, at, chips, False)
    entering = scan_states(
        gf, [vals[i * FWIDE : i * FWIDE + RHS, :] for i in range(STATE)], at, chips, False
    )
    vals[STATE * RHS : LANES, :] = none
    for i in range(STATE):
        vals[i * RHS : (i + 1) * RHS, :] = entering[i]
    pack(vals, ONE, s4, chips)
    post_state(s4, r4, 3)

    collect_map(s2, r2, MAP, 1, 0)
    unpack(r2, MAP, vals, chips)
    for i in range(STATE):
        gb[0, i] = vals[i * GWIDE : (i + 1) * GWIDE, :]
    scan_maps(gb, at, chips, True)
    collect_map(s3, r3, FULL, 2, 1)
    unpack(r3, FULL, vals, chips)
    state = []
    for i in range(STATE):
        acc = vals[i * FWIDE : i * FWIDE + RHS, :]
        for j in range(STATE):
            acc = acc + row(vals, i * FWIDE + RHS + j) * entering[j]
        state.append(acc)
    following = scan_states(gb, state, at, chips, True)
    vals[STATE * RHS : LANES, :] = none
    for i in range(STATE):
        vals[i * RHS : (i + 1) * RHS, :] = following[i]
    pack(vals, ONE, s5, chips)
    post_state(s5, r5, 4)

    collect_state(s4, r4, 3)
    unpack(r4, ONE, vals, nodes)

    def states():
        return [[vals[i * RHS : (i + 1) * RHS, :]] for i in range(STATE)]

    @pl.when(core == 0)
    def _():
        heads = chunks(mine_f, (0,))
        between = times(entry(mine_f, RHS), states(), lambda i: heads[i])
        heads = chunks(other_m, (0,))
        for i, (value,) in enumerate(times(entry(other_m, RHS), between, lambda i: heads[i])):
            follows[i] = value
        for i, (value,) in enumerate(states()):
            enters[i] = value

    @pl.when(core == 1)
    def _():
        heads = chunks(other_f, (0,))
        for i, (value,) in enumerate(times(entry(other_f, RHS), states(), lambda i: heads[i])):
            enters[i] = value

    entering = [enters[i] for i in range(STATE)]

    def enter(b, carry):
        for i in range(VARS):
            acc = zm[b, i, chunk(0), :]
            for j in range(STATE):
                acc = acc + row(zm, b, i, RHS + j) * entering[j]
            zpad[b, i] = acc
        return carry

    lax.fori_loop(0, blocks, enter, 0)
    collect_state(s5, r5, 4)
    unpack(r5, ONE, vals, nodes)

    @pl.when(core == 0)
    def _():
        for i, (value,) in enumerate(
            times(entry(other_b, 0), states(), lambda i: [follows[i]])
        ):
            follows[i] = value

    @pl.when(core == 1)
    def _():
        for i, (value,) in enumerate(states()):
            follows[i] = value

    following = [follows[i] for i in range(STATE)]
    for d in range(1, REACH + 1):
        for v in range(VARS):
            zpad[blocks - 1 + d, v] = following[(d - 1) * VARS + v]

    def follow(b, carry):
        for i in range(VARS):
            acc = zpad[b, i]
            for j in range(STATE):
                acc = acc + row(zb, b, i, j) * following[j]
            zpad[b, i] = acc
        return carry

    lax.fori_loop(0, blocks, follow, 0)
    rows_of = zpad.reshape(zpad.shape[0] * VARS * RHS, LANES)
    for tile in range(RHS):
        columns = rows_of[tile * LANES : (tile + 1) * LANES, :].T
        edges[0, tile : tile + 1, :] = columns[0:1]
        edges[1, tile : tile + 1, :] = columns[LANES - 1 :]
    left, right = lax.rem(sub + subs - 1, subs), lax.rem(sub + 1, subs)
    halo = [
        remote(edges.at[1], beside.at[0], 5, {"sub": right}),
        remote(edges.at[0], beside.at[1], 6, {"sub": left}),
        remote(upad.at[pl.ds(blocks, REACH)], before, 7, around(1)),
    ]
    halo[0].start()
    halo[1].start()
    store_corr = pltpu.make_async_copy(zpad.at[pl.ds(0, blocks)], corr_out, out_sem.at[0])
    store_corr.start()

    def difference(step, carry):
        b = blocks - 1 - step

        def emit(i, t, value):
            upad[b + REACH, i] = value

        at = upper(b)
        values = [[[zpad[at[k], j]] for j in range(VARS)] for k in range(SLOTS)]
        coupled(aup, b, values, emit)
        return carry

    lax.fori_loop(0, REACH, difference, 0)
    halo[2].start()
    lax.fori_loop(REACH, blocks, difference, 0)

    def apply(coef, b, i, values):
        total = None
        for k, column in enumerate(values):
            acc = None
            for j in range(VARS):
                term = row(coef, b * PAIR + (i * VARS + j) * SLOTS + k) * column[j]
                acc = term if acc is None else acc + term
            total = acc if total is None else total + acc
        return total

    def before_part(b, carry):
        at = lower(b)
        values = [[upad[at[k], j] for j in range(VARS)] for k in range(SLOTS)]
        for i in range(VARS):
            resid[b, i] = apply(low, b, i, values)
        return carry

    lax.fori_loop(REACH, blocks, before_part, 0)
    loads[4].wait()

    def inner_part(b, carry):
        west, east = [], []
        for j in range(VARS):
            value = zpad[b, j]
            west.append(jnp.where(lane == 0, 0.0, pltpu.roll(value, 1, 1)))
            east.append(jnp.where(lane == LANES - 1, 0.0, pltpu.roll(value, LANES - 1, 1)))
        for i in range(VARS):
            sided[b, i] = apply(side, b, i, (west, east))
        return carry

    def inner_parts(n, carry):
        for m in range(UNROLL):
            inner_part(n * UNROLL + m, carry)
        return carry

    lax.fori_loop(0, blocks // UNROLL, inner_parts, 0)
    halo[2].wait_recv()
    for d in range(REACH):
        for v in range(VARS):
            upad[d, v] = jnp.where(me == 0, 0.0, before[d, v])
    lax.fori_loop(0, REACH, before_part, 0)
    halo[0].wait_recv()
    halo[1].wait_recv()
    whole_row = (LANES, LANES)
    index = lax.broadcasted_iota(jnp.int32, whole_row, 0)
    for tile in range(RHS):
        west = jnp.where(sub == 0, 0.0, beside[0, tile : tile + 1, :])
        east = jnp.where(sub == subs - 1, 0.0, beside[1, tile : tile + 1, :])
        rows = jnp.where(
            index == 0,
            jnp.broadcast_to(west, whole_row),
            jnp.where(index == LANES - 1, jnp.broadcast_to(east, whole_row), 0.0),
        )
        outer[tile * LANES : (tile + 1) * LANES, :] = rows.T

    def edge_part(b, square):
        edge = [
            outer[pl.ds(pl.multiple_of((b * VARS + j) * RHS, RHS), RHS), :] for j in range(VARS)
        ]
        for i in range(VARS):
            value = resid[b, i] - sided[b, i]
            acc = None
            for j in range(VARS):
                at = b * PAIR + (i * VARS + j) * SLOTS
                term = jnp.where(lane == 0, row(side, at), row(side, at + 1)) * edge[j]
                acc = term if acc is None else acc + term
            value = value - acc
            resid[b, i] = value
            square = square + value * value
        return square

    def edge_parts(n, square):
        for m in range(UNROLL):
            square = edge_part(n * UNROLL + m, square)
        return square

    square = lax.fori_loop(0, blocks // UNROLL, edge_parts, none)
    store_resid = pltpu.make_async_copy(resid, resid_out, out_sem.at[1])
    store_resid.start()
    sums = jnp.sum(square, axis=1, keepdims=True)
    diagonal = lax.broadcasted_iota(jnp.int32, (RHS, LANES), 0) == lane
    part[...] = jnp.sum(jnp.where(diagonal, sums, 0.0), axis=0, keepdims=True)

    rounds = ((along, line, place, part, wide, stage), (cross, across, flat, stage, deep, total))
    for n, (peer, count, index, src, dst, out) in enumerate(rounds):

        def tell(k, carry, peer=peer, src=src, dst=dst, index=index, n=n):
            remote(src, dst.at[index], 8 + n, peer(k)).start()
            return carry

        lax.fori_loop(1, count, tell, 0)
        mine_too = pltpu.make_async_copy(src, dst.at[index], own_sem.at[5 + n])
        mine_too.start()
        mine_too.wait()
        rows = pl.ds(0, count - 1)
        remote(dst.at[rows], dst.at[rows], 8 + n, peer(1)).wait_recv()
        out[...] = jnp.sum(dst[...], axis=0)

    store_corr.wait()
    store_resid.wait()

    @pl.when(core == 0)
    def _():
        whole(s1, FULL, 0, nodes - 1).wait_send()
        whole(s2, MAP, 1, nodes - 1).wait_send()

    @pl.when(core == 1)
    def _():
        whole(s3, FULL, 2, nodes - 1).wait_send()

    for n, ref in ((3, r4), (4, r5)):
        whole(ref, ONE, n, nodes - 1).wait_send()
    for copy in pairs:
        copy.wait_send()
    for copy in halo:
        copy.wait_send()
    for n, (peer, count, _, _, dst, _) in enumerate(rounds):
        rows = pl.ds(0, count - 1)
        remote(dst.at[rows], dst.at[rows], 8 + n, peer(1)).wait_send()


def scale_kernel(entries, corr, resid, total, corr_out, out, held, piece, sums_in, load_sem, store_sem):
    parts = piece.shape[0] // 8
    rows = [pl.ds(8 * n, 8) for n in range(parts)]
    loads = [pltpu.make_async_copy(total, sums_in, load_sem.at[parts])]
    loads += [pltpu.make_async_copy(resid.at[r], piece.at[r], load_sem.at[n]) for n, r in enumerate(rows)]
    loads += [pltpu.make_async_copy(corr, held, load_sem.at[parts + 1])]
    stores = [pltpu.make_async_copy(piece.at[r], out.at[r], store_sem.at[n]) for n, r in enumerate(rows)]
    stores += [pltpu.make_async_copy(held, corr_out, store_sem.at[parts])]
    for load in loads:
        load.start()
    lane = lanes_of((RHS, LANES))
    diagonal = lax.broadcasted_iota(jnp.int32, (RHS, LANES), 0) == lane
    loads[0].wait()
    wide = jnp.broadcast_to(sums_in[...], (RHS, LANES))
    sums = jnp.sum(jnp.where(diagonal, wide, 0.0), axis=1, keepdims=True)
    factor = jnp.broadcast_to(lax.rsqrt(sums / entries + 1e-6), (RHS, LANES))
    for n, r in enumerate(rows):
        loads[1 + n].wait()
        piece[r] = piece[r] * factor[None, None]
        stores[n].start()
    loads[-1].wait()
    stores[-1].start()
    for store in stores:
        store.wait()


def spec(space):
    return pl.BlockSpec(memory_space=space)


def shards(nodes, subs, line, rhs, diag_block, diag_inverse, lower_coef, upper_coef, side_coef, lower_cols, upper_cols, counts):
    blocks = rhs.shape[0]
    cells = rhs.shape[3]
    padded = blocks + REACH + 1
    across = subs * (nodes // line)
    dinv = jnp.transpose(diag_inverse, (1, 2, 0, 3)).reshape(VARS * VARS, blocks, cells)
    low, up, side = (
        jnp.transpose(x, (0, 2, 3, 1, 4)).reshape(blocks * PAIR, cells)
        for x in (lower_coef, upper_coef, side_coef)
    )
    plane = jax.ShapeDtypeStruct((blocks, VARS, RHS, cells), F32)
    slots = VMEM((nodes * SLOT, cells), F32)
    window = VMEM((padded, VARS, RHS, cells), F32)
    half_slots = VMEM((nodes // 2 * SLOT, cells), F32)
    depth = len(shifts(nodes // 2))
    corr, resid, total = pl.pallas_call(
        functools.partial(main_kernel, nodes, subs, line),
        out_shape=(plane, plane, jax.ShapeDtypeStruct((1, cells), F32)),
        in_specs=[spec(pl.ANY)] * 8,
        out_specs=(spec(pl.ANY), spec(pl.ANY), spec(VMEM)),
        scratch_shapes=[pltpu.SMEM((SLOTS, blocks), jnp.int32)] * 3
        + [VMEM(plane.shape, F32)] * 2
        + [VMEM(x.shape, F32) for x in (rhs, dinv, low, up, side)]
        + [VMEM((PAIR, blocks, cells), F32)] * 2
        + [VMEM((padded, VARS, wide, cells), F32) for wide in (FWIDE, GWIDE, FWIDE)]
        + [VMEM((FULL * LANES, cells), F32)]
        + [slots] * 5
        + [half_slots] * 5
        + [VMEM((depth, STATE, GWIDE, cells), F32)] * 2
        + [VMEM((REACH, VARS, wide, cells), F32) for wide in (FWIDE, GWIDE, FWIDE)]
        + [VMEM((STATE, wide, cells), F32) for wide in (FWIDE, RHS, RHS)]
        + [window] * 2
        + [VMEM((REACH, VARS, RHS, cells), F32)]
        + [VMEM((RHS * LANES, cells), F32)]
        + [VMEM((2, RHS, cells), F32)] * 2
        + [VMEM((1, cells), F32)] * 2
        + [VMEM((line, 1, cells), F32), VMEM((across, 1, cells), F32)]
        + [pltpu.SemaphoreType.DMA((n,)) for n in (8, 13, 13, 7, 2)],
        compiler_params=pltpu.CompilerParams(
            collective_id=0, has_side_effects=True, vmem_limit_bytes=VMEM_LIMIT
        ),
        name="sweeps",
    )(lower_cols.T, upper_cols.T, counts.T, rhs, dinv, low, up, side)
    entries = nodes * blocks * VARS * subs * cells
    return pl.pallas_call(
        functools.partial(scale_kernel, entries),
        out_shape=(plane, plane),
        in_specs=[spec(pl.ANY)] * 3,
        out_specs=(spec(pl.ANY),) * 2,
        scratch_shapes=[VMEM(plane.shape, F32)] * 2
        + [VMEM((1, cells), F32)]
        + [pltpu.SemaphoreType.DMA((blocks // 8 + n,)) for n in (2, 1)],
        compiler_params=pltpu.CompilerParams(vmem_limit_bytes=VMEM_LIMIT),
        name="scale",
    )(corr, resid, total)


def solution(mesh):
    nodes, subs = mesh.shape["chain"], mesh.shape["sub"]
    line = 16 if nodes % 16 == 0 else nodes
    plane = P("chain", None, None, "sub")
    coef = P("chain", None, None, None, "sub")
    return jax.shard_map(
        functools.partial(shards, nodes, subs, line),
        mesh=mesh,
        in_specs=(plane, plane, plane, coef, coef, coef, P("chain", None), P("chain", None), P("chain", None)),
        out_specs=(plane, plane),
        check_vma=False,
    )
```

```python
import functools

import jax
import jax.numpy as jnp
from jax import lax
from jax.experimental import pallas as pl
from jax.experimental.pallas import tpu as pltpu
from jax.sharding import PartitionSpec as P

VARS = 5
RHS = 8
REACH = 3
SLOTS = 2
STATE = REACH * VARS
LANES = 128
PAIR = VARS * VARS * SLOTS
FWIDE = 24
GWIDE = 16
SLOT = 8
FULL, MAP, ONE = 3, 2, 1
F32 = jnp.float32
VMEM = pltpu.VMEM
MESH = pl.DeviceIdType.MESH
VMEM_LIMIT = 61 << 20
UNROLL = 4


def row(ref, *index):
    *lead, at = index
    return ref[(*lead, pl.ds(at, RHS, stride=0), slice(None))]


def lanes_of(shape):
    return lax.broadcasted_iota(jnp.int32, shape, len(shape) - 1)


def chunk(t):
    return slice(8 * t, 8 * t + 8)


def near(cols, counts, side, slot, b, start, forward, absent):
    col = cols[slot, b] - start
    used = slot < counts[side, b]
    return jnp.where(used, col + REACH if forward else col, absent)


def couple(coef, dinv, out, blocks):
    for group in range(blocks // 8):
        rows = pl.ds(8 * group, 8)
        inv = [dinv[q, rows, :] for q in range(VARS * VARS)]
        for slot in range(SLOTS):
            for j in range(VARS):
                col = [
                    coef[pl.ds(8 * group * PAIR + (m * VARS + j) * SLOTS + slot, 8, stride=PAIR), :]
                    for m in range(VARS)
                ]
                for i in range(VARS):
                    acc = inv[i * VARS] * col[0]
                    for m in range(1, VARS):
                        acc = acc + inv[i * VARS + m] * col[m]
                    out[slot * 25 + i * VARS + j, rows, :] = acc


def coupled(coef, b, values, emit):
    for i in range(VARS):
        part = []
        for k in range(SLOTS):
            acc = None
            for j in range(VARS):
                c = row(coef, k * 25 + i * VARS + j, b)
                new = [c * x for x in values[k][j]]
                acc = new if acc is None else [p + q for p, q in zip(acc, new)]
            part.append(acc)
        for t, (p, q) in enumerate(zip(*part)):
            emit(i, t, p + q)


def pack(vals, tiles, send, span):
    for tile in range(tiles):
        turned = vals[tile * LANES : (tile + 1) * LANES, :].T
        for c in range(2):
            for first in range(0, span, 8):
                at = first * SLOT + c * tiles + tile
                send[pl.ds(at, 8, stride=SLOT), :] = turned[c * span + first : c * span + first + 8]


def each(low, high, step):
    count = high - low
    some = next(n for n in (8, 5, 4, 3, 1) if count % n == 0)

    def trip(n, carry):
        for m in range(some):
            step(low + n * some + m)
        return carry

    lax.fori_loop(0, count // some, trip, 0)


def unpack(recv, tiles, vals, span):
    for tile in range(tiles):
        both = [recv[pl.ds(c * tiles + tile, span, stride=SLOT), :] for c in range(2)]
        both = both * (LANES // (2 * span))
        vals[tile * LANES : (tile + 1) * LANES, :] = jnp.concatenate(both, 0).T


def times(coef, values, start):
    out = []
    for i in range(STATE):
        acc = list(start(i))
        for j in range(STATE):
            c = coef(i, j)
            acc = [c * x if a is None else a + c * x for a, x in zip(acc, values[j])]
        out.append(acc)
    return out


def shifts(span):
    return [1 << n for n in range(span.bit_length() - 1)]


def turned(x, shift, ahead):
    return pltpu.roll(x, LANES - shift if ahead else shift, 1)


def scan_maps(stack, lane, span, ahead):
    for n, shift in enumerate(shifts(span)[:-1]):
        inside = lane < span - shift if ahead else lane >= shift
        for t in range(2):
            e = [turned(stack[n, j, chunk(t), :], shift, ahead) for j in range(STATE)]
            for i in range(STATE):
                acc = None
                for j in range(STATE):
                    term = row(stack, n, i, j) * e[j]
                    acc = term if acc is None else acc + term
                stack[n + 1, i, chunk(t), :] = jnp.where(inside, acc, stack[n, i, chunk(t), :])


def scan_states(stack, state, lane, span, ahead):
    for n, shift in enumerate(shifts(span)):
        inside = lane < span - shift if ahead else lane >= shift
        e = [turned(x, shift, ahead) for x in state]
        fresh = []
        for i in range(STATE):
            acc = state[i]
            for j in range(STATE):
                acc = acc + row(stack, n, i, j) * e[j]
            fresh.append(jnp.where(inside, acc, state[i]))
        state = fresh
    edge = lane == span - 1 if ahead else lane == 0
    return [jnp.where(edge, 0.0, turned(x, 1, ahead)) for x in state]


def main_kernel(
    nodes, subs, line, lcol_in, ucol_in, counts_in, rhs_in, dinv_in, low_in, up_in, side_in,
    corr_out, resid_out, total,
    lcol, ucol, counts, resid, sided, rhs, dinv, low, up, side, alow, aup, y, zb, zm, vals,
    s1, s2, s3, r4, r5, r1, r2, r3, s4, s5, gf, gb, yp, zbp, zmp, mid, enters, follows,
    zpad, upad, before, outer, edges, beside, part, stage, wide, deep,
    load_sem, send_sem, recv_sem, own_sem, out_sem,
):
    blocks = rhs.shape[0]
    me, sub = lax.axis_index("chain"), lax.axis_index("sub")
    start, absent = me * blocks, blocks + REACH
    loads = [
        pltpu.make_async_copy(src, dst, load_sem.at[n])
        for n, (src, dst) in enumerate(
            (
                (low_in, low), (dinv_in, dinv), (rhs_in, rhs), (up_in, up), (side_in, side),
                (lcol_in, lcol), (ucol_in, ucol), (counts_in, counts),
            )
        )
    ]
    for load in loads:
        load.start()

    barrier = pltpu.get_barrier_semaphore()
    flat = (me // line) * subs + sub
    place = lax.rem(me, line)

    def cross(k):
        other = lax.rem(flat + k, subs * (nodes // line))
        return {"chain": (other // subs) * line + place, "sub": lax.rem(other, subs)}

    def along(k):
        return {"chain": me - place + lax.rem(place + k, line)}

    def around(k):
        return {"chain": lax.rem(me + k, nodes)}

    across = subs * (nodes // line)
    spans = ((nodes // 2, nodes), (nodes // 4, nodes // 2), (1, nodes // 4))
    for peer, spans_of in ((around, spans[:1]), (cross, ((1, across),)), (around, spans[1:])):
        for low_k, high_k in spans_of:

            def greet(k, peer=peer):
                pl.semaphore_signal(barrier, inc=1, device_id=peer(k), device_id_type=MESH)

            each(low_k, high_k, greet)

    def remote(src, dst, n, peer):
        return pltpu.make_async_remote_copy(
            src_ref=src,
            dst_ref=dst,
            send_sem=send_sem.at[n],
            recv_sem=recv_sem.at[n],
            device_id=peer,
            device_id_type=MESH,
        )

    chips, chip, core = nodes // 2, me // 2, lax.rem(me, 2)

    def slot(n, tiles):
        return pl.ds(pl.multiple_of(n * SLOT, SLOT), 2 * tiles)

    def own(src, dst, tiles, n, out, inside):
        return pltpu.make_async_copy(src.at[slot(out, tiles)], dst.at[slot(inside, tiles)], own_sem.at[n])

    def post(src, dst, tiles, n, out, inside):
        own(src, dst, tiles, n, out(me), inside).start()

        def one(k):
            to = lax.rem(me + k, nodes)
            remote(src.at[slot(out(to), tiles)], dst.at[slot(inside, tiles)], n, {"chain": to}).start()

        for low_k, high_k in spans:
            each(low_k, high_k, one)

    def whole(ref, tiles, n, count):
        rows = pl.ds(0, 2 * tiles * count)
        return remote(ref.at[rows], ref.at[rows], n, around(1))

    def post_map(src, dst, tiles, n):
        post(src, dst, tiles, n, lambda to: to, chip)

    def post_state(src, dst, n):
        post(src, dst, ONE, n, lambda to: to // 2, me)

    def collect_map(src, dst, tiles, n, sender):
        @pl.when(core == sender)
        def _():
            own(src, dst, tiles, n, me, chip).wait()
            whole(dst, tiles, n, chips - 1).wait_recv()

        @pl.when(core != sender)
        def _():
            whole(dst, tiles, n, chips).wait_recv()

    def collect_state(src, dst, n):
        own(src, dst, ONE, n, chip, me).wait()
        whole(dst, ONE, n, nodes - 1).wait_recv()

    fsub = lax.broadcasted_iota(jnp.int32, (FWIDE, LANES), 0)
    gsub = lax.broadcasted_iota(jnp.int32, (GWIDE, LANES), 0)
    for d in range(1, REACH + 1):
        for v in range(VARS):
            q = (d - 1) * VARS + v
            y[REACH - d, v] = jnp.where(fsub == RHS + q, 1.0, 0.0).astype(F32)
            zb[blocks - 1 + d, v] = jnp.where(gsub == q, 1.0, 0.0).astype(F32)
            zm[blocks - 1 + d, v] = jnp.zeros((FWIDE, LANES), F32)
    none = jnp.zeros((RHS, LANES), F32)
    for v in range(VARS):
        y[absent, v] = jnp.zeros((FWIDE, LANES), F32)
        zm[absent, v] = jnp.zeros((FWIDE, LANES), F32)
        zb[absent, v] = jnp.zeros((GWIDE, LANES), F32)
        zpad[absent, v] = none
        upad[absent, v] = none
    vals[...] = jnp.zeros(vals.shape, F32)

    def lower(b):
        return [near(lcol, counts, 0, k, b, start, True, absent) for k in range(SLOTS)]

    def upper(b):
        return [near(ucol, counts, 1, k, b, start, False, absent) for k in range(SLOTS)]

    def window(ref, at, chunks):
        return [
            [[ref[at[k], j, chunk(t), :] for t in range(chunks)] for j in range(VARS)]
            for k in range(SLOTS)
        ]

    for n in (5, 6, 7, 0, 1):
        loads[n].wait()
    couple(low, dinv, alow, blocks)
    loads[3].wait()
    couple(up, dinv, aup, blocks)
    loads[2].wait()

    def forward(b):
        values = window(y, lower(b), 3)
        src = [rhs[b, m] for m in range(VARS)]
        own_part = []
        for i in range(VARS):
            w = row(dinv, i * VARS, b) * src[0]
            for m in range(1, VARS):
                w = w + row(dinv, i * VARS + m, b) * src[m]
            own_part.append(w)

        def emit(i, t, value):
            y[b + REACH, i, chunk(t), :] = own_part[i] - value if t == 0 else -value

        coupled(alow, b, values, emit)

    def basis(b):

        def emit(i, t, value):
            zb[b, i, chunk(t), :] = -value

        coupled(aup, b, window(zb, upper(b), 2), emit)

    def both_ways(b, carry):
        forward(b)
        basis(blocks - 1 - b)
        return carry

    lax.fori_loop(0, blocks, both_ways, 0)

    def backward(step, carry):
        b = blocks - 1 - step

        def emit(i, t, value):
            zm[b, i, chunk(t), :] = y[b + REACH, i, chunk(t), :] - value

        coupled(aup, b, window(zm, upper(b), 3), emit)
        return carry

    lax.fori_loop(0, blocks, backward, 0)
    pl.semaphore_wait(barrier, nodes + across - 2)

    partner = {"chain": me + 1 - 2 * core}
    ends = (y.at[pl.ds(blocks, REACH)], zb.at[pl.ds(0, REACH)], zm.at[pl.ds(0, REACH)])
    pairs = [
        remote(src, dst, 10 + n, partner) for n, (src, dst) in enumerate(zip(ends, (yp, zbp, zmp)))
    ]
    for copy in pairs:
        copy.start()

    def at_state(q):
        return q // VARS, q % VARS

    def forward_at(ref, last):
        def index(q):
            d, v = at_state(q)
            return ref, last - d, v

        return index

    def backward_at(ref):
        def index(q):
            d, v = at_state(q)
            return ref, d, v

        return index

    def chunks(index, span):
        parts = []
        for q in range(STATE):
            ref, d, v = index(q)
            parts.append([ref[d, v, chunk(t), :] for t in span])
        return parts

    def entry(index, offset):
        def coef(i, j):
            ref, d, v = index(i)
            return row(ref, d, v, offset + j)

        return coef

    mine_f, mine_b, mine_m = forward_at(y, blocks + REACH - 1), backward_at(zb), backward_at(zm)
    other_f, other_b, other_m = forward_at(yp, REACH - 1), backward_at(zbp), backward_at(zmp)

    def put(out, wide, parts):
        for i, part in enumerate(parts):
            for t, value in enumerate(part):
                out[i * wide + 8 * t : i * wide + 8 * t + 8, :] = value

    pairs[0].wait_recv()

    @pl.when(core == 0)
    def _():
        heads = chunks(other_f, (0,))
        for t in range(3):
            values = chunks(mine_f, (t,))
            start_of = (lambda i: heads[i]) if t == 0 else (lambda i: [None])
            for i, (value,) in enumerate(times(entry(other_f, RHS), values, start_of)):
                vals[i * FWIDE + 8 * t : i * FWIDE + 8 * t + 8, :] = value
        pack(vals, FULL, s1, nodes)
        post_map(s1, r1, FULL, 0)
        pairs[1].wait_recv()
        values = chunks(other_b, (0, 1))
        put(vals, GWIDE, times(entry(mine_b, 0), values, lambda i: [None, None]))
        pack(vals, MAP, s2, nodes)
        post_map(s2, r2, MAP, 1)
        pairs[2].wait_recv()

    @pl.when(core == 1)
    def _():
        heads = chunks(mine_m, (0,))
        for t in range(3):
            values = chunks(other_f, (t,))
            start_of = (lambda i: heads[i]) if t == 0 else (lambda i: [None])
            for i, (value,) in enumerate(times(entry(mine_m, RHS), values, start_of)):
                mid[i, chunk(t), :] = value
        pairs[1].wait_recv()
        pairs[2].wait_recv()
        for t in range(3):
            values = [[mid[j, chunk(t), :]] for j in range(STATE)]
            heads = chunks(other_m, (t,))
            for i, (value,) in enumerate(times(entry(other_b, 0), values, lambda i: heads[i])):
                vals[i * FWIDE + 8 * t : i * FWIDE + 8 * t + 8, :] = value
        pack(vals, FULL, s3, nodes)
        post_map(s3, r3, FULL, 2)

    lane = lanes_of((RHS, LANES))
    at = lax.rem(lane, chips)
    collect_map(s1, r1, FULL, 0, 0)
    unpack(r1, FULL, vals, chips)
    for i in range(STATE):
        gf[0, i] = vals[i * FWIDE + RHS : (i + 1) * FWIDE, :]
    scan_maps(gf, at, chips, False)
    entering = scan_states(
        gf, [vals[i * FWIDE : i * FWIDE + RHS, :] for i in range(STATE)], at, chips, False
    )
    vals[STATE * RHS : LANES, :] = none
    for i in range(STATE):
        vals[i * RHS : (i + 1) * RHS, :] = entering[i]
    pack(vals, ONE, s4, chips)
    post_state(s4, r4, 3)

    collect_map(s2, r2, MAP, 1, 0)
    unpack(r2, MAP, vals, chips)
    for i in range(STATE):
        gb[0, i] = vals[i * GWIDE : (i + 1) * GWIDE, :]
    scan_maps(gb, at, chips, True)
    collect_map(s3, r3, FULL, 2, 1)
    unpack(r3, FULL, vals, chips)
    state = []
    for i in range(STATE):
        acc = vals[i * FWIDE : i * FWIDE + RHS, :]
        for j in range(STATE):
            acc = acc + row(vals, i * FWIDE + RHS + j) * entering[j]
        state.append(acc)
    following = scan_states(gb, state, at, chips, True)
    vals[STATE * RHS : LANES, :] = none
    for i in range(STATE):
        vals[i * RHS : (i + 1) * RHS, :] = following[i]
    pack(vals, ONE, s5, chips)
    post_state(s5, r5, 4)

    collect_state(s4, r4, 3)
    unpack(r4, ONE, vals, nodes)

    def states():
        return [[vals[i * RHS : (i + 1) * RHS, :]] for i in range(STATE)]

    @pl.when(core == 0)
    def _():
        heads = chunks(mine_f, (0,))
        between = times(entry(mine_f, RHS), states(), lambda i: heads[i])
        heads = chunks(other_m, (0,))
        for i, (value,) in enumerate(times(entry(other_m, RHS), between, lambda i: heads[i])):
            follows[i] = value
        for i, (value,) in enumerate(states()):
            enters[i] = value

    @pl.when(core == 1)
    def _():
        heads = chunks(other_f, (0,))
        for i, (value,) in enumerate(times(entry(other_f, RHS), states(), lambda i: heads[i])):
            enters[i] = value

    entering = [enters[i] for i in range(STATE)]

    def enter(b, carry):
        for i in range(VARS):
            acc = zm[b, i, chunk(0), :]
            for j in range(STATE):
                acc = acc + row(zm, b, i, RHS + j) * entering[j]
            zpad[b, i] = acc
        return carry

    lax.fori_loop(0, blocks, enter, 0)
    collect_state(s5, r5, 4)
    unpack(r5, ONE, vals, nodes)

    @pl.when(core == 0)
    def _():
        for i, (value,) in enumerate(
            times(entry(other_b, 0), states(), lambda i: [follows[i]])
        ):
            follows[i] = value

    @pl.when(core == 1)
    def _():
        for i, (value,) in enumerate(states()):
            follows[i] = value

    following = [follows[i] for i in range(STATE)]
    for d in range(1, REACH + 1):
        for v in range(VARS):
            zpad[blocks - 1 + d, v] = following[(d - 1) * VARS + v]

    def follow(b):
        for i in range(VARS):
            acc = zpad[b, i]
            for j in range(STATE):
                acc = acc + row(zb, b, i, j) * following[j]
            zpad[b, i] = acc

    each(0, blocks, follow)
    rows_of = zpad.reshape(zpad.shape[0] * VARS * RHS, LANES)
    for tile in range(RHS):
        columns = rows_of[tile * LANES : (tile + 1) * LANES, :].T
        edges[0, tile : tile + 1, :] = columns[0:1]
        edges[1, tile : tile + 1, :] = columns[LANES - 1 :]
    left, right = lax.rem(sub + subs - 1, subs), lax.rem(sub + 1, subs)
    halo = [
        remote(edges.at[1], beside.at[0], 5, {"sub": right}),
        remote(edges.at[0], beside.at[1], 6, {"sub": left}),
        remote(upad.at[pl.ds(blocks, REACH)], before, 7, around(1)),
    ]
    halo[0].start()
    halo[1].start()

    def difference(b):

        def emit(i, t, value):
            upad[b + REACH, i] = value

        at = upper(b)
        values = [[[zpad[at[k], j]] for j in range(VARS)] for k in range(SLOTS)]
        coupled(aup, b, values, emit)

    each(blocks - REACH, blocks, difference)
    halo[2].start()
    store_corr = pltpu.make_async_copy(zpad.at[pl.ds(0, blocks)], corr_out, out_sem.at[0])
    store_corr.start()
    each(0, blocks - REACH, difference)

    def apply(coef, b, i, values):
        total = None
        for k, column in enumerate(values):
            acc = None
            for j in range(VARS):
                term = row(coef, b * PAIR + (i * VARS + j) * SLOTS + k) * column[j]
                acc = term if acc is None else acc + term
            total = acc if total is None else total + acc
        return total

    def before_part(b):
        at = lower(b)
        values = [[upad[at[k], j] for j in range(VARS)] for k in range(SLOTS)]
        for i in range(VARS):
            resid[b, i] = apply(low, b, i, values)

    loads[4].wait()

    def inner_part(b):
        west, east = [], []
        for j in range(VARS):
            value = zpad[b, j]
            west.append(jnp.where(lane == 0, 0.0, pltpu.roll(value, 1, 1)))
            east.append(jnp.where(lane == LANES - 1, 0.0, pltpu.roll(value, LANES - 1, 1)))
        for i in range(VARS):
            sided[b, i] = apply(side, b, i, (west, east))

    def inside(b):
        before_part(b)
        inner_part(b)

    each(REACH, blocks, inside)
    each(0, REACH, inner_part)
    halo[2].wait_recv()
    for d in range(REACH):
        for v in range(VARS):
            upad[d, v] = jnp.where(me == 0, 0.0, before[d, v])
    each(0, REACH, before_part)
    halo[0].wait_recv()
    halo[1].wait_recv()
    whole_row = (LANES, LANES)
    index = lax.broadcasted_iota(jnp.int32, whole_row, 0)
    for tile in range(RHS):
        west = jnp.where(sub == 0, 0.0, beside[0, tile : tile + 1, :])
        east = jnp.where(sub == subs - 1, 0.0, beside[1, tile : tile + 1, :])
        rows = jnp.where(
            index == 0,
            jnp.broadcast_to(west, whole_row),
            jnp.where(index == LANES - 1, jnp.broadcast_to(east, whole_row), 0.0),
        )
        outer[tile * LANES : (tile + 1) * LANES, :] = rows.T

    def edge_part(b, square):
        edge = [
            outer[pl.ds(pl.multiple_of((b * VARS + j) * RHS, RHS), RHS), :] for j in range(VARS)
        ]
        for i in range(VARS):
            value = resid[b, i] - sided[b, i]
            acc = None
            for j in range(VARS):
                at = b * PAIR + (i * VARS + j) * SLOTS
                term = jnp.where(lane == 0, row(side, at), row(side, at + 1)) * edge[j]
                acc = term if acc is None else acc + term
            value = value - acc
            resid[b, i] = value
            square = square + value * value
        return square

    def edge_parts(n, square):
        for m in range(UNROLL):
            square = edge_part(n * UNROLL + m, square)
        return square

    square = lax.fori_loop(0, blocks // UNROLL, edge_parts, none)
    store_resid = pltpu.make_async_copy(resid, resid_out, out_sem.at[1])
    store_resid.start()
    sums = jnp.sum(square, axis=1, keepdims=True)
    diagonal = lax.broadcasted_iota(jnp.int32, (RHS, LANES), 0) == lane
    part[...] = jnp.sum(jnp.where(diagonal, sums, 0.0), axis=0, keepdims=True)

    rounds = ((along, line, place, part, wide, stage), (cross, across, flat, stage, deep, total))
    for n, (peer, count, index, src, dst, out) in enumerate(rounds):

        def tell(k, peer=peer, src=src, dst=dst, index=index, n=n):
            remote(src, dst.at[index], 8 + n, peer(k)).start()

        each(1, count, tell)
        mine_too = pltpu.make_async_copy(src, dst.at[index], own_sem.at[5 + n])
        mine_too.start()
        mine_too.wait()
        rows = pl.ds(0, count - 1)
        remote(dst.at[rows], dst.at[rows], 8 + n, peer(1)).wait_recv()
        out[...] = jnp.sum(dst[...], axis=0)

    store_corr.wait()
    store_resid.wait()

    @pl.when(core == 0)
    def _():
        whole(s1, FULL, 0, nodes - 1).wait_send()
        whole(s2, MAP, 1, nodes - 1).wait_send()

    @pl.when(core == 1)
    def _():
        whole(s3, FULL, 2, nodes - 1).wait_send()

    for n, ref in ((3, r4), (4, r5)):
        whole(ref, ONE, n, nodes - 1).wait_send()
    for copy in pairs:
        copy.wait_send()
    for copy in halo:
        copy.wait_send()
    for n, (peer, count, _, _, dst, _) in enumerate(rounds):
        rows = pl.ds(0, count - 1)
        remote(dst.at[rows], dst.at[rows], 8 + n, peer(1)).wait_send()


def scale_kernel(entries, corr, resid, total, corr_out, out, held, piece, sums_in, load_sem, store_sem):
    parts = piece.shape[0] // 8
    rows = [pl.ds(8 * n, 8) for n in range(parts)]
    loads = [pltpu.make_async_copy(total, sums_in, load_sem.at[parts])]
    loads += [pltpu.make_async_copy(resid.at[r], piece.at[r], load_sem.at[n]) for n, r in enumerate(rows)]
    loads += [pltpu.make_async_copy(corr, held, load_sem.at[parts + 1])]
    stores = [pltpu.make_async_copy(piece.at[r], out.at[r], store_sem.at[n]) for n, r in enumerate(rows)]
    stores += [pltpu.make_async_copy(held, corr_out, store_sem.at[parts])]
    for load in loads:
        load.start()
    lane = lanes_of((RHS, LANES))
    diagonal = lax.broadcasted_iota(jnp.int32, (RHS, LANES), 0) == lane
    loads[0].wait()
    wide = jnp.broadcast_to(sums_in[...], (RHS, LANES))
    sums = jnp.sum(jnp.where(diagonal, wide, 0.0), axis=1, keepdims=True)
    factor = jnp.broadcast_to(lax.rsqrt(sums / entries + 1e-6), (RHS, LANES))
    for n, r in enumerate(rows):
        loads[1 + n].wait()
        piece[r] = piece[r] * factor[None, None]
        stores[n].start()
    loads[-1].wait()
    stores[-1].start()
    for store in stores:
        store.wait()


def spec(space):
    return pl.BlockSpec(memory_space=space)


def shards(nodes, subs, line, rhs, diag_block, diag_inverse, lower_coef, upper_coef, side_coef, lower_cols, upper_cols, counts):
    blocks = rhs.shape[0]
    cells = rhs.shape[3]
    padded = blocks + REACH + 1
    across = subs * (nodes // line)
    dinv = jnp.transpose(diag_inverse, (1, 2, 0, 3)).reshape(VARS * VARS, blocks, cells)
    low, up, side = (
        jnp.transpose(x, (0, 2, 3, 1, 4)).reshape(blocks * PAIR, cells)
        for x in (lower_coef, upper_coef, side_coef)
    )
    plane = jax.ShapeDtypeStruct((blocks, VARS, RHS, cells), F32)
    slots = VMEM((nodes * SLOT, cells), F32)
    window = VMEM((padded, VARS, RHS, cells), F32)
    half_slots = VMEM((nodes // 2 * SLOT, cells), F32)
    depth = len(shifts(nodes // 2))
    corr, resid, total = pl.pallas_call(
        functools.partial(main_kernel, nodes, subs, line),
        out_shape=(plane, plane, jax.ShapeDtypeStruct((1, cells), F32)),
        in_specs=[spec(pl.ANY)] * 8,
        out_specs=(spec(pl.ANY), spec(pl.ANY), spec(VMEM)),
        scratch_shapes=[pltpu.SMEM((SLOTS, blocks), jnp.int32)] * 3
        + [VMEM(plane.shape, F32)] * 2
        + [VMEM(x.shape, F32) for x in (rhs, dinv, low, up, side)]
        + [VMEM((PAIR, blocks, cells), F32)] * 2
        + [VMEM((padded, VARS, wide, cells), F32) for wide in (FWIDE, GWIDE, FWIDE)]
        + [VMEM((FULL * LANES, cells), F32)]
        + [slots] * 5
        + [half_slots] * 5
        + [VMEM((depth, STATE, GWIDE, cells), F32)] * 2
        + [VMEM((REACH, VARS, wide, cells), F32) for wide in (FWIDE, GWIDE, FWIDE)]
        + [VMEM((STATE, wide, cells), F32) for wide in (FWIDE, RHS, RHS)]
        + [window] * 2
        + [VMEM((REACH, VARS, RHS, cells), F32)]
        + [VMEM((RHS * LANES, cells), F32)]
        + [VMEM((2, RHS, cells), F32)] * 2
        + [VMEM((1, cells), F32)] * 2
        + [VMEM((line, 1, cells), F32), VMEM((across, 1, cells), F32)]
        + [pltpu.SemaphoreType.DMA((n,)) for n in (8, 13, 13, 7, 2)],
        compiler_params=pltpu.CompilerParams(
            collective_id=0, has_side_effects=True, vmem_limit_bytes=VMEM_LIMIT
        ),
        name="sweeps",
    )(lower_cols.T, upper_cols.T, counts.T, rhs, dinv, low, up, side)
    entries = nodes * blocks * VARS * subs * cells
    return pl.pallas_call(
        functools.partial(scale_kernel, entries),
        out_shape=(plane, plane),
        in_specs=[spec(pl.ANY)] * 3,
        out_specs=(spec(pl.ANY),) * 2,
        scratch_shapes=[VMEM(plane.shape, F32)] * 2
        + [VMEM((1, cells), F32)]
        + [pltpu.SemaphoreType.DMA((blocks // 8 + n,)) for n in (2, 1)],
        compiler_params=pltpu.CompilerParams(vmem_limit_bytes=VMEM_LIMIT),
        name="scale",
    )(corr, resid, total)


def solution(mesh):
    nodes, subs = mesh.shape["chain"], mesh.shape["sub"]
    line = 16 if nodes % 16 == 0 else nodes
    plane = P("chain", None, None, "sub")
    coef = P("chain", None, None, None, "sub")
    return jax.shard_map(
        functools.partial(shards, nodes, subs, line),
        mesh=mesh,
        in_specs=(plane, plane, plane, coef, coef, coef, P("chain", None), P("chain", None), P("chain", None)),
        out_specs=(plane, plane),
        check_vma=False,
    )
```

```python
import functools

import jax
import jax.numpy as jnp
from jax import lax
from jax.experimental import pallas as pl
from jax.experimental.pallas import tpu as pltpu
from jax.sharding import PartitionSpec as P

VARS = 5
RHS = 8
REACH = 3
SLOTS = 2
STATE = REACH * VARS
LANES = 128
PAIR = VARS * VARS * SLOTS
FWIDE = 24
GWIDE = 16
SLOT = 8
FULL, MAP, ONE = 3, 2, 1
F32 = jnp.float32
VMEM = pltpu.VMEM
MESH = pl.DeviceIdType.MESH
VMEM_LIMIT = 61 << 20
UNROLL = 4


def row(ref, *index):
    *lead, at = index
    return ref[(*lead, pl.ds(at, RHS, stride=0), slice(None))]


def lanes_of(shape):
    return lax.broadcasted_iota(jnp.int32, shape, len(shape) - 1)


def chunk(t):
    return slice(8 * t, 8 * t + 8)


def near(cols, counts, side, slot, b, start, forward, absent):
    col = cols[slot, b] - start
    used = slot < counts[side, b]
    return jnp.where(used, col + REACH if forward else col, absent)


def couple(coef, dinv, out, blocks):
    for group in range(blocks // 8):
        rows = pl.ds(8 * group, 8)
        inv = [dinv[q, rows, :] for q in range(VARS * VARS)]
        for slot in range(SLOTS):
            for j in range(VARS):
                col = [
                    coef[pl.ds(8 * group * PAIR + (m * VARS + j) * SLOTS + slot, 8, stride=PAIR), :]
                    for m in range(VARS)
                ]
                for i in range(VARS):
                    acc = inv[i * VARS] * col[0]
                    for m in range(1, VARS):
                        acc = acc + inv[i * VARS + m] * col[m]
                    out[slot * 25 + i * VARS + j, rows, :] = acc


def coupled(coef, b, values, emit):
    for i in range(VARS):
        part = []
        for k in range(SLOTS):
            acc = None
            for j in range(VARS):
                c = row(coef, k * 25 + i * VARS + j, b)
                new = [c * x for x in values[k][j]]
                acc = new if acc is None else [p + q for p, q in zip(acc, new)]
            part.append(acc)
        for t, (p, q) in enumerate(zip(*part)):
            emit(i, t, p + q)


def pack(vals, tiles, send, span):
    for tile in range(tiles):
        turned = vals[tile * LANES : (tile + 1) * LANES, :].T
        for c in range(2):
            for first in range(0, span, 8):
                at = first * SLOT + c * tiles + tile
                send[pl.ds(at, 8, stride=SLOT), :] = turned[c * span + first : c * span + first + 8]


def each(low, high, step):
    count = high - low
    some = next(n for n in (8, 5, 4, 3, 1) if count % n == 0)

    def trip(n, carry):
        for m in range(some):
            step(low + n * some + m)
        return carry

    lax.fori_loop(0, count // some, trip, 0)


def unpack(recv, tiles, vals, span):
    for tile in range(tiles):
        both = [recv[pl.ds(c * tiles + tile, span, stride=SLOT), :] for c in range(2)]
        both = both * (LANES // (2 * span))
        vals[tile * LANES : (tile + 1) * LANES, :] = jnp.concatenate(both, 0).T


def times(coef, values, start):
    out = []
    for i in range(STATE):
        acc = list(start(i))
        for j in range(STATE):
            c = coef(i, j)
            acc = [c * x if a is None else a + c * x for a, x in zip(acc, values[j])]
        out.append(acc)
    return out


def shifts(span):
    return [1 << n for n in range(span.bit_length() - 1)]


def turned(x, shift, ahead):
    return pltpu.roll(x, LANES - shift if ahead else shift, 1)


def scan_maps(stack, lane, span, ahead):
    for n, shift in enumerate(shifts(span)[:-1]):
        inside = lane < span - shift if ahead else lane >= shift
        for t in range(2):
            e = [turned(stack[n, j, chunk(t), :], shift, ahead) for j in range(STATE)]
            for i in range(STATE):
                acc = None
                for j in range(STATE):
                    term = row(stack, n, i, j) * e[j]
                    acc = term if acc is None else acc + term
                stack[n + 1, i, chunk(t), :] = jnp.where(inside, acc, stack[n, i, chunk(t), :])


def scan_states(stack, state, lane, span, ahead):
    for n, shift in enumerate(shifts(span)):
        inside = lane < span - shift if ahead else lane >= shift
        e = [turned(x, shift, ahead) for x in state]
        fresh = []
        for i in range(STATE):
            acc = state[i]
            for j in range(STATE):
                acc = acc + row(stack, n, i, j) * e[j]
            fresh.append(jnp.where(inside, acc, state[i]))
        state = fresh
    edge = lane == span - 1 if ahead else lane == 0
    return [jnp.where(edge, 0.0, turned(x, 1, ahead)) for x in state]


def main_kernel(
    nodes, subs, line, lcol_in, ucol_in, counts_in, rhs_in, dinv_in, low_in, up_in, side_in,
    corr_out, resid, total,
    lcol, ucol, counts, sided, rhs, dinv, low, up, side, alow, aup, y, zb, zm, vals,
    s1, s2, s3, r4, r5, r1, r2, r3, s4, s5, gf, gb, yp, zbp, zmp, mid, enters, follows,
    zpad, upad, before, outer, edges, beside, part, stage, wide, deep,
    load_sem, send_sem, recv_sem, own_sem, out_sem,
):
    blocks = rhs.shape[0]
    me, sub = lax.axis_index("chain"), lax.axis_index("sub")
    start, absent = me * blocks, blocks + REACH
    loads = [
        pltpu.make_async_copy(src, dst, load_sem.at[n])
        for n, (src, dst) in enumerate(
            (
                (low_in, low), (dinv_in, dinv), (rhs_in, rhs), (up_in, up), (side_in, side),
                (lcol_in, lcol), (ucol_in, ucol), (counts_in, counts),
            )
        )
    ]
    for load in loads:
        load.start()

    barrier = pltpu.get_barrier_semaphore()
    flat = (me // line) * subs + sub
    place = lax.rem(me, line)

    def cross(k):
        other = lax.rem(flat + k, subs * (nodes // line))
        return {"chain": (other // subs) * line + place, "sub": lax.rem(other, subs)}

    def along(k):
        return {"chain": me - place + lax.rem(place + k, line)}

    def around(k):
        return {"chain": lax.rem(me + k, nodes)}

    across = subs * (nodes // line)
    spans = ((nodes // 2, nodes), (nodes // 4, nodes // 2), (1, nodes // 4))
    for peer, spans_of in ((around, spans[:1]), (cross, ((1, across),)), (around, spans[1:])):
        for low_k, high_k in spans_of:

            def greet(k, peer=peer):
                pl.semaphore_signal(barrier, inc=1, device_id=peer(k), device_id_type=MESH)

            each(low_k, high_k, greet)

    def remote(src, dst, n, peer):
        return pltpu.make_async_remote_copy(
            src_ref=src,
            dst_ref=dst,
            send_sem=send_sem.at[n],
            recv_sem=recv_sem.at[n],
            device_id=peer,
            device_id_type=MESH,
        )

    chips, chip, core = nodes // 2, me // 2, lax.rem(me, 2)

    def slot(n, tiles):
        return pl.ds(pl.multiple_of(n * SLOT, SLOT), 2 * tiles)

    def own(src, dst, tiles, n, out, inside):
        return pltpu.make_async_copy(src.at[slot(out, tiles)], dst.at[slot(inside, tiles)], own_sem.at[n])

    def post(src, dst, tiles, n, out, inside):
        own(src, dst, tiles, n, out(me), inside).start()

        def one(k):
            to = lax.rem(me + k, nodes)
            remote(src.at[slot(out(to), tiles)], dst.at[slot(inside, tiles)], n, {"chain": to}).start()

        for low_k, high_k in spans:
            each(low_k, high_k, one)

    def whole(ref, tiles, n, count):
        rows = pl.ds(0, 2 * tiles * count)
        return remote(ref.at[rows], ref.at[rows], n, around(1))

    def post_map(src, dst, tiles, n):
        post(src, dst, tiles, n, lambda to: to, chip)

    def post_state(src, dst, n):
        post(src, dst, ONE, n, lambda to: to // 2, me)

    def collect_map(src, dst, tiles, n, sender):
        @pl.when(core == sender)
        def _():
            own(src, dst, tiles, n, me, chip).wait()
            whole(dst, tiles, n, chips - 1).wait_recv()

        @pl.when(core != sender)
        def _():
            whole(dst, tiles, n, chips).wait_recv()

    def collect_state(src, dst, n):
        own(src, dst, ONE, n, chip, me).wait()
        whole(dst, ONE, n, nodes - 1).wait_recv()

    fsub = lax.broadcasted_iota(jnp.int32, (FWIDE, LANES), 0)
    gsub = lax.broadcasted_iota(jnp.int32, (GWIDE, LANES), 0)
    for d in range(1, REACH + 1):
        for v in range(VARS):
            q = (d - 1) * VARS + v
            y[REACH - d, v] = jnp.where(fsub == RHS + q, 1.0, 0.0).astype(F32)
            zb[blocks - 1 + d, v] = jnp.where(gsub == q, 1.0, 0.0).astype(F32)
            zm[blocks - 1 + d, v] = jnp.zeros((FWIDE, LANES), F32)
    none = jnp.zeros((RHS, LANES), F32)
    for v in range(VARS):
        y[absent, v] = jnp.zeros((FWIDE, LANES), F32)
        zm[absent, v] = jnp.zeros((FWIDE, LANES), F32)
        zb[absent, v] = jnp.zeros((GWIDE, LANES), F32)
        zpad[absent, v] = none
        upad[absent, v] = none
    vals[...] = jnp.zeros(vals.shape, F32)

    def lower(b):
        return [near(lcol, counts, 0, k, b, start, True, absent) for k in range(SLOTS)]

    def upper(b):
        return [near(ucol, counts, 1, k, b, start, False, absent) for k in range(SLOTS)]

    def window(ref, at, chunks):
        return [
            [[ref[at[k], j, chunk(t), :] for t in range(chunks)] for j in range(VARS)]
            for k in range(SLOTS)
        ]

    for n in (5, 6, 7, 0, 1):
        loads[n].wait()
    couple(low, dinv, alow, blocks)
    loads[3].wait()
    couple(up, dinv, aup, blocks)
    loads[2].wait()

    def forward(b):
        values = window(y, lower(b), 3)
        src = [rhs[b, m] for m in range(VARS)]
        own_part = []
        for i in range(VARS):
            w = row(dinv, i * VARS, b) * src[0]
            for m in range(1, VARS):
                w = w + row(dinv, i * VARS + m, b) * src[m]
            own_part.append(w)

        def emit(i, t, value):
            y[b + REACH, i, chunk(t), :] = own_part[i] - value if t == 0 else -value

        coupled(alow, b, values, emit)

    def basis(b):

        def emit(i, t, value):
            zb[b, i, chunk(t), :] = -value

        coupled(aup, b, window(zb, upper(b), 2), emit)

    def both_ways(b, carry):
        forward(b)
        basis(blocks - 1 - b)
        return carry

    lax.fori_loop(0, blocks, both_ways, 0)

    def backward(step, carry):
        b = blocks - 1 - step

        def emit(i, t, value):
            zm[b, i, chunk(t), :] = y[b + REACH, i, chunk(t), :] - value

        coupled(aup, b, window(zm, upper(b), 3), emit)
        return carry

    lax.fori_loop(0, blocks, backward, 0)
    pl.semaphore_wait(barrier, nodes + across - 2)

    partner = {"chain": me + 1 - 2 * core}
    ends = (y.at[pl.ds(blocks, REACH)], zb.at[pl.ds(0, REACH)], zm.at[pl.ds(0, REACH)])
    pairs = [
        remote(src, dst, 10 + n, partner) for n, (src, dst) in enumerate(zip(ends, (yp, zbp, zmp)))
    ]
    for copy in pairs:
        copy.start()

    def at_state(q):
        return q // VARS, q % VARS

    def forward_at(ref, last):
        def index(q):
            d, v = at_state(q)
            return ref, last - d, v

        return index

    def backward_at(ref):
        def index(q):
            d, v = at_state(q)
            return ref, d, v

        return index

    def chunks(index, span):
        parts = []
        for q in range(STATE):
            ref, d, v = index(q)
            parts.append([ref[d, v, chunk(t), :] for t in span])
        return parts

    def entry(index, offset):
        def coef(i, j):
            ref, d, v = index(i)
            return row(ref, d, v, offset + j)

        return coef

    mine_f, mine_b, mine_m = forward_at(y, blocks + REACH - 1), backward_at(zb), backward_at(zm)
    other_f, other_b, other_m = forward_at(yp, REACH - 1), backward_at(zbp), backward_at(zmp)

    def put(out, wide, parts):
        for i, part in enumerate(parts):
            for t, value in enumerate(part):
                out[i * wide + 8 * t : i * wide + 8 * t + 8, :] = value

    pairs[0].wait_recv()

    @pl.when(core == 0)
    def _():
        heads = chunks(other_f, (0,))
        for t in range(3):
            values = chunks(mine_f, (t,))
            start_of = (lambda i: heads[i]) if t == 0 else (lambda i: [None])
            for i, (value,) in enumerate(times(entry(other_f, RHS), values, start_of)):
                vals[i * FWIDE + 8 * t : i * FWIDE + 8 * t + 8, :] = value
        pack(vals, FULL, s1, nodes)
        post_map(s1, r1, FULL, 0)
        pairs[1].wait_recv()
        values = chunks(other_b, (0, 1))
        put(vals, GWIDE, times(entry(mine_b, 0), values, lambda i: [None, None]))
        pack(vals, MAP, s2, nodes)
        post_map(s2, r2, MAP, 1)
        pairs[2].wait_recv()

    @pl.when(core == 1)
    def _():
        heads = chunks(mine_m, (0,))
        for t in range(3):
            values = chunks(other_f, (t,))
            start_of = (lambda i: heads[i]) if t == 0 else (lambda i: [None])
            for i, (value,) in enumerate(times(entry(mine_m, RHS), values, start_of)):
                mid[i, chunk(t), :] = value
        pairs[1].wait_recv()
        pairs[2].wait_recv()
        for t in range(3):
            values = [[mid[j, chunk(t), :]] for j in range(STATE)]
            heads = chunks(other_m, (t,))
            for i, (value,) in enumerate(times(entry(other_b, 0), values, lambda i: heads[i])):
                vals[i * FWIDE + 8 * t : i * FWIDE + 8 * t + 8, :] = value
        pack(vals, FULL, s3, nodes)
        post_map(s3, r3, FULL, 2)

    lane = lanes_of((RHS, LANES))
    at = lax.rem(lane, chips)
    collect_map(s1, r1, FULL, 0, 0)
    unpack(r1, FULL, vals, chips)
    for i in range(STATE):
        gf[0, i] = vals[i * FWIDE + RHS : (i + 1) * FWIDE, :]
    scan_maps(gf, at, chips, False)
    entering = scan_states(
        gf, [vals[i * FWIDE : i * FWIDE + RHS, :] for i in range(STATE)], at, chips, False
    )
    vals[STATE * RHS : LANES, :] = none
    for i in range(STATE):
        vals[i * RHS : (i + 1) * RHS, :] = entering[i]
    pack(vals, ONE, s4, chips)
    post_state(s4, r4, 3)

    collect_map(s2, r2, MAP, 1, 0)
    unpack(r2, MAP, vals, chips)
    for i in range(STATE):
        gb[0, i] = vals[i * GWIDE : (i + 1) * GWIDE, :]
    scan_maps(gb, at, chips, True)
    collect_map(s3, r3, FULL, 2, 1)
    unpack(r3, FULL, vals, chips)
    state = []
    for i in range(STATE):
        acc = vals[i * FWIDE : i * FWIDE + RHS, :]
        for j in range(STATE):
            acc = acc + row(vals, i * FWIDE + RHS + j) * entering[j]
        state.append(acc)
    following = scan_states(gb, state, at, chips, True)
    vals[STATE * RHS : LANES, :] = none
    for i in range(STATE):
        vals[i * RHS : (i + 1) * RHS, :] = following[i]
    pack(vals, ONE, s5, chips)
    post_state(s5, r5, 4)

    collect_state(s4, r4, 3)
    unpack(r4, ONE, vals, nodes)

    def states():
        return [[vals[i * RHS : (i + 1) * RHS, :]] for i in range(STATE)]

    @pl.when(core == 0)
    def _():
        heads = chunks(mine_f, (0,))
        between = times(entry(mine_f, RHS), states(), lambda i: heads[i])
        heads = chunks(other_m, (0,))
        for i, (value,) in enumerate(times(entry(other_m, RHS), between, lambda i: heads[i])):
            follows[i] = value
        for i, (value,) in enumerate(states()):
            enters[i] = value

    @pl.when(core == 1)
    def _():
        heads = chunks(other_f, (0,))
        for i, (value,) in enumerate(times(entry(other_f, RHS), states(), lambda i: heads[i])):
            enters[i] = value

    entering = [enters[i] for i in range(STATE)]

    def enter(b, carry):
        for i in range(VARS):
            acc = zm[b, i, chunk(0), :]
            for j in range(STATE):
                acc = acc + row(zm, b, i, RHS + j) * entering[j]
            zpad[b, i] = acc
        return carry

    lax.fori_loop(0, blocks, enter, 0)
    collect_state(s5, r5, 4)
    unpack(r5, ONE, vals, nodes)

    @pl.when(core == 0)
    def _():
        for i, (value,) in enumerate(
            times(entry(other_b, 0), states(), lambda i: [follows[i]])
        ):
            follows[i] = value

    @pl.when(core == 1)
    def _():
        for i, (value,) in enumerate(states()):
            follows[i] = value

    following = [follows[i] for i in range(STATE)]
    for d in range(1, REACH + 1):
        for v in range(VARS):
            zpad[blocks - 1 + d, v] = following[(d - 1) * VARS + v]

    def follow(b):
        for i in range(VARS):
            acc = zpad[b, i]
            for j in range(STATE):
                acc = acc + row(zb, b, i, j) * following[j]
            zpad[b, i] = acc

    each(0, blocks, follow)
    rows_of = zpad.reshape(zpad.shape[0] * VARS * RHS, LANES)
    for tile in range(RHS):
        columns = rows_of[tile * LANES : (tile + 1) * LANES, :].T
        edges[0, tile : tile + 1, :] = columns[0:1]
        edges[1, tile : tile + 1, :] = columns[LANES - 1 :]
    left, right = lax.rem(sub + subs - 1, subs), lax.rem(sub + 1, subs)
    halo = [
        remote(edges.at[1], beside.at[0], 5, {"sub": right}),
        remote(edges.at[0], beside.at[1], 6, {"sub": left}),
        remote(upad.at[pl.ds(blocks, REACH)], before, 7, around(1)),
    ]
    halo[0].start()
    halo[1].start()

    def difference(b):

        def emit(i, t, value):
            upad[b + REACH, i] = value

        at = upper(b)
        values = [[[zpad[at[k], j]] for j in range(VARS)] for k in range(SLOTS)]
        coupled(aup, b, values, emit)

    each(blocks - REACH, blocks, difference)
    halo[2].start()
    store_corr = pltpu.make_async_copy(zpad.at[pl.ds(0, blocks)], corr_out, out_sem.at[0])
    store_corr.start()
    each(0, blocks - REACH, difference)

    def apply(coef, b, i, values):
        total = None
        for k, column in enumerate(values):
            acc = None
            for j in range(VARS):
                term = row(coef, b * PAIR + (i * VARS + j) * SLOTS + k) * column[j]
                acc = term if acc is None else acc + term
            total = acc if total is None else total + acc
        return total

    def before_part(b):
        at = lower(b)
        values = [[upad[at[k], j] for j in range(VARS)] for k in range(SLOTS)]
        for i in range(VARS):
            resid[b, i] = apply(low, b, i, values)

    loads[4].wait()

    def inner_part(b):
        west, east = [], []
        for j in range(VARS):
            value = zpad[b, j]
            west.append(jnp.where(lane == 0, 0.0, pltpu.roll(value, 1, 1)))
            east.append(jnp.where(lane == LANES - 1, 0.0, pltpu.roll(value, LANES - 1, 1)))
        for i in range(VARS):
            sided[b, i] = apply(side, b, i, (west, east))

    def inside(b):
        before_part(b)
        inner_part(b)

    each(REACH, blocks, inside)
    each(0, REACH, inner_part)
    halo[2].wait_recv()
    for d in range(REACH):
        for v in range(VARS):
            upad[d, v] = jnp.where(me == 0, 0.0, before[d, v])
    each(0, REACH, before_part)
    halo[0].wait_recv()
    halo[1].wait_recv()
    whole_row = (LANES, LANES)
    index = lax.broadcasted_iota(jnp.int32, whole_row, 0)
    for tile in range(RHS):
        west = jnp.where(sub == 0, 0.0, beside[0, tile : tile + 1, :])
        east = jnp.where(sub == subs - 1, 0.0, beside[1, tile : tile + 1, :])
        rows = jnp.where(
            index == 0,
            jnp.broadcast_to(west, whole_row),
            jnp.where(index == LANES - 1, jnp.broadcast_to(east, whole_row), 0.0),
        )
        outer[tile * LANES : (tile + 1) * LANES, :] = rows.T

    def edge_part(b, square):
        edge = [
            outer[pl.ds(pl.multiple_of((b * VARS + j) * RHS, RHS), RHS), :] for j in range(VARS)
        ]
        for i in range(VARS):
            value = resid[b, i] - sided[b, i]
            acc = None
            for j in range(VARS):
                at = b * PAIR + (i * VARS + j) * SLOTS
                term = jnp.where(lane == 0, row(side, at), row(side, at + 1)) * edge[j]
                acc = term if acc is None else acc + term
            value = value - acc
            resid[b, i] = value
            square = square + value * value
        return square

    def edge_parts(n, square):
        for m in range(UNROLL):
            square = edge_part(n * UNROLL + m, square)
        return square

    square = lax.fori_loop(0, blocks // UNROLL, edge_parts, none)
    sums = jnp.sum(square, axis=1, keepdims=True)
    diagonal = lax.broadcasted_iota(jnp.int32, (RHS, LANES), 0) == lane
    part[...] = jnp.sum(jnp.where(diagonal, sums, 0.0), axis=0, keepdims=True)

    rounds = ((along, line, place, part, wide, stage), (cross, across, flat, stage, deep, total))
    for n, (peer, count, index, src, dst, out) in enumerate(rounds):

        def tell(k, peer=peer, src=src, dst=dst, index=index, n=n):
            remote(src, dst.at[index], 8 + n, peer(k)).start()

        each(1, count, tell)
        mine_too = pltpu.make_async_copy(src, dst.at[index], own_sem.at[5 + n])
        mine_too.start()
        mine_too.wait()
        rows = pl.ds(0, count - 1)
        remote(dst.at[rows], dst.at[rows], 8 + n, peer(1)).wait_recv()
        out[...] = jnp.sum(dst[...], axis=0)

    store_corr.wait()

    @pl.when(core == 0)
    def _():
        whole(s1, FULL, 0, nodes - 1).wait_send()
        whole(s2, MAP, 1, nodes - 1).wait_send()

    @pl.when(core == 1)
    def _():
        whole(s3, FULL, 2, nodes - 1).wait_send()

    for n, ref in ((3, r4), (4, r5)):
        whole(ref, ONE, n, nodes - 1).wait_send()
    for copy in pairs:
        copy.wait_send()
    for copy in halo:
        copy.wait_send()
    for n, (peer, count, _, _, dst, _) in enumerate(rounds):
        rows = pl.ds(0, count - 1)
        remote(dst.at[rows], dst.at[rows], 8 + n, peer(1)).wait_send()


def scale_kernel(entries, corr, resid, total, corr_out, out, scaled, store_sem):
    parts = scaled.shape[0] // 8
    rows = [pl.ds(8 * n, 8) for n in range(parts)]
    stores = [pltpu.make_async_copy(scaled.at[r], out.at[r], store_sem.at[n]) for n, r in enumerate(rows)]
    stores += [pltpu.make_async_copy(corr, corr_out, store_sem.at[parts])]
    stores[-1].start()
    lane = lanes_of((RHS, LANES))
    diagonal = lax.broadcasted_iota(jnp.int32, (RHS, LANES), 0) == lane
    wide = jnp.broadcast_to(total[...], (RHS, LANES))
    sums = jnp.sum(jnp.where(diagonal, wide, 0.0), axis=1, keepdims=True)
    factor = jnp.broadcast_to(lax.rsqrt(sums / entries + 1e-6), (RHS, LANES))
    for n, r in enumerate(rows):
        scaled[r] = resid[r] * factor[None, None]
        stores[n].start()
    for store in stores:
        store.wait()


def spec(space):
    return pl.BlockSpec(memory_space=space)


def shards(nodes, subs, line, rhs, diag_block, diag_inverse, lower_coef, upper_coef, side_coef, lower_cols, upper_cols, counts):
    blocks = rhs.shape[0]
    cells = rhs.shape[3]
    padded = blocks + REACH + 1
    across = subs * (nodes // line)
    dinv = jnp.transpose(diag_inverse, (1, 2, 0, 3)).reshape(VARS * VARS, blocks, cells)
    low, up, side = (
        jnp.transpose(x, (0, 2, 3, 1, 4)).reshape(blocks * PAIR, cells)
        for x in (lower_coef, upper_coef, side_coef)
    )
    plane = jax.ShapeDtypeStruct((blocks, VARS, RHS, cells), F32)
    slots = VMEM((nodes * SLOT, cells), F32)
    window = VMEM((padded, VARS, RHS, cells), F32)
    half_slots = VMEM((nodes // 2 * SLOT, cells), F32)
    depth = len(shifts(nodes // 2))
    corr, resid, total = pl.pallas_call(
        functools.partial(main_kernel, nodes, subs, line),
        out_shape=(VMEM(plane.shape, F32), VMEM(plane.shape, F32), VMEM((1, cells), F32)),
        in_specs=[spec(pl.ANY)] * 8,
        out_specs=(spec(VMEM),) * 3,
        scratch_shapes=[pltpu.SMEM((SLOTS, blocks), jnp.int32)] * 3
        + [VMEM(plane.shape, F32)]
        + [VMEM(x.shape, F32) for x in (rhs, dinv, low, up, side)]
        + [VMEM((PAIR, blocks, cells), F32)] * 2
        + [VMEM((padded, VARS, wide, cells), F32) for wide in (FWIDE, GWIDE, FWIDE)]
        + [VMEM((FULL * LANES, cells), F32)]
        + [slots] * 5
        + [half_slots] * 5
        + [VMEM((depth, STATE, GWIDE, cells), F32)] * 2
        + [VMEM((REACH, VARS, wide, cells), F32) for wide in (FWIDE, GWIDE, FWIDE)]
        + [VMEM((STATE, wide, cells), F32) for wide in (FWIDE, RHS, RHS)]
        + [window] * 2
        + [VMEM((REACH, VARS, RHS, cells), F32)]
        + [VMEM((RHS * LANES, cells), F32)]
        + [VMEM((2, RHS, cells), F32)] * 2
        + [VMEM((1, cells), F32)] * 2
        + [VMEM((line, 1, cells), F32), VMEM((across, 1, cells), F32)]
        + [pltpu.SemaphoreType.DMA((n,)) for n in (8, 13, 13, 7, 1)],
        compiler_params=pltpu.CompilerParams(
            collective_id=0, has_side_effects=True, vmem_limit_bytes=VMEM_LIMIT
        ),
        name="sweeps",
    )(lower_cols.T, upper_cols.T, counts.T, rhs, dinv, low, up, side)
    entries = nodes * blocks * VARS * subs * cells
    return pl.pallas_call(
        functools.partial(scale_kernel, entries),
        out_shape=(plane, plane),
        in_specs=[spec(VMEM)] * 3,
        out_specs=(spec(pl.ANY),) * 2,
        scratch_shapes=[VMEM(plane.shape, F32), pltpu.SemaphoreType.DMA((blocks // 8 + 1,))],
        compiler_params=pltpu.CompilerParams(vmem_limit_bytes=8 << 20),
        name="scale",
    )(corr, resid, total)


def solution(mesh):
    nodes, subs = mesh.shape["chain"], mesh.shape["sub"]
    line = 16 if nodes % 16 == 0 else nodes
    plane = P("chain", None, None, "sub")
    coef = P("chain", None, None, None, "sub")
    return jax.shard_map(
        functools.partial(shards, nodes, subs, line),
        mesh=mesh,
        in_specs=(plane, plane, plane, coef, coef, coef, P("chain", None), P("chain", None), P("chain", None)),
        out_specs=(plane, plane),
        check_vma=False,
    )
```
